128 devices in a mesh: wide: 16 (over y, z), narrow: 8 (over x, core).
Axes of the slice: x: 4, y: 4, z: 4, core: 2. Of those that a mesh axis runs over, the one named last changes fastest.
Arguments:
- adjoint: float32 [3, 512, 256, 256], P(None, 'wide', 'narrow'), may hold values from -6 to 6
- velocity: float32 [3, 512, 256, 256], P(None, 'wide', 'narrow'), may hold values from -6 to 6
- deriv_x: float32 [256, 256], replicated, as said below
- deriv_y: float32 [256, 256], replicated, as said below
- deriv_z: float32 [512, 512], replicated, as said below
- rotor_blocks: int32 [96, 64], replicated, may hold values from 0 to 262143, as said below
- turbine_owner: int32 [96], replicated, may hold values from 0 to 127, as said below
- disk_weight: float32 [96, 64, 128], replicated, may hold values from 0.1 to 1
- thrust: float32 [96], replicated, may hold values from 0.5 to 2
Outputs:
- updated_adjoint: float32 [3, 512, 256, 256], P(None, 'wide', 'narrow')
- turbine_grad: float32 [256, 2], P(('wide', 'narrow'))
The draws below stay inside these ranges and needn't reach their ends.
Inputs may be any that keep to these rules, and one draw needn't show every extreme that they name: `deriv_x`: entries vanish where the row's block of 64 and the column's block differ by more than one. `deriv_y`: entries vanish where the row's block of 32 and the column's block differ by more than one. `deriv_z`: entries vanish where the row's block of 16 and the column's block differ by more than one. `rotor_blocks`: block id b = (z * 256 + y) * 2 + x block. A rotor's row lists 64 // 2 consecutive z planes times 2 consecutive y lines, all at one x block, z major. `turbine_owner`: devices are numbered wide major over wide and narrow. No device owns more than 2 turbines, and one owns exactly 2.
All inputs are finite; a program needn't handle non-finite values.
Results may differ from the reference program's by a relative error of at most 0.00014.
Values sent between devices are 32-bit elements; how exact they have to be, the bound alone decides.
No kernel may reach another device: no remote copies, remote signals or barrier semaphores. Data moves between devices by JAX's collectives and lax.ppermute only.
A program may use at most 192 MiB of HBM per device.

```python
import math
import jax
import jax.numpy as jnp
from jax import lax

NX = 256
NY = 256
NZ = 512
BX = 64
BY = 32
BAND = 16
RY = 2
TURB = 96
ROTOR = 64
SLOTS = 2
DEVICES = 128


def band_matrix(key, order, block):
    row_block = jnp.arange(order)[:, None] // block
    col_block = jnp.arange(order)[None, :] // block
    in_band = (jnp.abs(row_block - col_block) <= 1).astype(jnp.float32)
    values = jax.random.normal(key, (order, order), jnp.float32)
    return values * in_band / jnp.sqrt(3.0 * block)


def draw_deriv_x(key, part):
    return band_matrix(jax.random.fold_in(key, 11), NX, BX)


def draw_deriv_y(key, part):
    return band_matrix(jax.random.fold_in(key, 12), NY, BY)


def draw_deriv_z(key, part):
    return band_matrix(jax.random.fold_in(key, 13), NZ, BAND)


def draw_rotor_blocks(key, part):
    key_z, key_y, key_x = jax.random.split(jax.random.fold_in(key, 21), 3)
    extent_z = ROTOR // RY
    x_blocks = NX // 128
    turbine = jnp.arange(TURB)
    start_z = jax.random.randint(key_z, (TURB,), 0, NZ - extent_z + 1)
    start_y = jax.random.randint(key_y, (TURB,), 0, NY - RY + 1)
    start_x = jax.random.randint(key_x, (TURB,), 0, x_blocks)
    start_z = jnp.where(turbine == 0, 0, jnp.where(turbine == 1, NZ - extent_z, start_z))
    start_y = jnp.where(turbine == 0, 0, jnp.where(turbine == 1, NY - RY, start_y))
    start_x = jnp.where(turbine == 0, 0, jnp.where(turbine == 1, x_blocks - 1, start_x))
    offset_z = jnp.arange(ROTOR) // RY
    offset_y = jnp.arange(ROTOR) % RY
    blocks = ((start_z[:, None] + offset_z[None, :]) * NY + start_y[:, None] + offset_y[None, :]) * x_blocks + start_x[:, None]
    return blocks.astype(jnp.int32)


def place_value(shuffled, wanted, target_slot):
    found_at = jnp.argmax((shuffled == wanted).astype(jnp.int32))
    previous = shuffled[target_slot]
    return shuffled.at[found_at].set(previous).at[target_slot].set(wanted)


def draw_turbine_owner(key, part):
    shuffled = jax.random.permutation(jax.random.fold_in(key, 31), DEVICES).astype(jnp.int32)
    shuffled = place_value(shuffled, 0, 2)
    shuffled = place_value(shuffled, DEVICES - 1, 1)
    turbine = jnp.arange(TURB)
    pick_index = jnp.where(turbine == TURB - 1, 0, turbine % DEVICES)
    return shuffled[pick_index].astype(jnp.int32)


def shard_levels(stream_key, extent, cuts, smallest, top_value):
    loudness, own = 1.0, jax.random.fold_in(stream_key, 6)
    for axis_at, shards_of in cuts:
        steps = jnp.exp(jax.random.uniform(jax.random.fold_in(own, axis_at), (shards_of,), jnp.float32, smallest / len(cuts), top_value / len(cuts)))
        loudness = loudness * jnp.repeat(steps, extent[axis_at] // shards_of).reshape([-1 if axis == axis_at else 1 for axis in range(len(extent))])
    return loudness


def gaussian(stream_key, shape, deviation, bound, cuts=(), kind=jnp.bfloat16):
    values = jax.random.normal(stream_key, shape, jnp.float32) * deviation
    if len(cuts) > 0:
        values = shard_levels(stream_key, shape, cuts, -0.22, 0.18) * values
    return jnp.clip(values, min=-bound, max=bound).astype(kind)


def setup_inputs(seed: int = 0) -> dict:
    key_list = jax.random.split(jax.random.key(seed), 10)
    adjoint = gaussian(key_list[0], (3, NZ, NY, NX), 1.0, 6.0, ((1, 16), (2, 8)), jnp.float32)
    velocity = gaussian(key_list[1], (3, NZ, NY, NX), 1.0, 6.0, ((1, 16), (2, 8)), jnp.float32)
    deriv_x = draw_deriv_x(jax.random.fold_in(key_list[9], 71), 0)
    deriv_y = draw_deriv_y(jax.random.fold_in(key_list[9], 71), 0)
    deriv_z = draw_deriv_z(jax.random.fold_in(key_list[9], 71), 0)
    rotor_blocks = draw_rotor_blocks(jax.random.fold_in(key_list[9], 71), 0)
    turbine_owner = draw_turbine_owner(jax.random.fold_in(key_list[9], 71), 0)
    disk_weight = jnp.clip(jnp.exp(jax.random.uniform(key_list[7], (TURB, ROTOR, 128), jnp.float32, math.log(0.1), math.log(1.0))), 0.1, 1.0)
    thrust = jnp.clip(jax.random.uniform(key_list[8], (TURB,), jnp.float32, 0.5, 2.0), 0.5, 2.0)
    return dict(adjoint=adjoint, velocity=velocity, deriv_x=deriv_x, deriv_y=deriv_y, deriv_z=deriv_z, rotor_blocks=rotor_blocks, turbine_owner=turbine_owner, disk_weight=disk_weight, thrust=thrust)


def directional(adjoint, velocity, adj_deriv, vel_deriv, direction):
    advect = velocity[direction][None] * adj_deriv
    stretch = -lax.optimization_barrier(jnp.sum(adjoint * vel_deriv, axis=0))
    select = (jnp.arange(3) == direction).astype(jnp.float32)[:, None, None, None]
    return advect + select * stretch[None]

def reference(adjoint, velocity, deriv_x, deriv_y, deriv_z, rotor_blocks, turbine_owner, disk_weight, thrust):
    highest = lax.Precision.HIGHEST
    tendency = jnp.zeros_like(adjoint)
    forms = (('czyk,xk->czyx', deriv_x), ('czkx,yk->czyx', deriv_y), ('ckyx,zk->czyx', deriv_z))
    for direction in range(3):
        form, matrix = forms[direction]
        adj_deriv = jnp.einsum(form, adjoint, matrix, precision=highest)
        vel_deriv = jnp.einsum(form, velocity, matrix, precision=highest)
        tendency = tendency + directional(adjoint, velocity, adj_deriv, vel_deriv, direction)
    x_blocks = NX // 128
    weighted = thrust[:, None, None] * disk_weight
    source = jnp.zeros((NZ * NY * x_blocks, 128), jnp.float32)
    source = source.at[rotor_blocks.reshape(-1)].add(weighted.reshape(-1, 128)).reshape(NZ, NY, NX)
    forcing = source * jnp.abs(velocity[0]) * adjoint[0]
    select = (jnp.arange(3) == 0).astype(jnp.float32)[:, None, None, None]
    tendency = tendency - select * forcing[None]
    updated = adjoint + 0.2 * tendency
    ax_rows = adjoint[0].reshape(-1, 128)[rotor_blocks]
    ay_rows = adjoint[1].reshape(-1, 128)[rotor_blocks]
    ux_rows = velocity[0].reshape(-1, 128)[rotor_blocks]
    thrust_drive = ux_rows * jnp.abs(ux_rows)
    scale = 1.0 / math.sqrt(128.0 * ROTOR)
    grad_thrust = lax.optimization_barrier(jnp.sum(disk_weight * ax_rows * thrust_drive, axis=(1, 2))) * scale
    grad_side = lax.optimization_barrier(jnp.sum(disk_weight * ay_rows * thrust_drive, axis=(1, 2))) * scale
    grad = jnp.stack([grad_thrust, grad_side], axis=1)
    positions = jnp.arange(TURB)
    shared = turbine_owner[:, None] == turbine_owner[None, :]
    earlier = positions[:, None] > positions[None, :]
    slot_rank = lax.optimization_barrier(jnp.sum((shared & earlier).astype(jnp.int32), axis=1)).astype(jnp.int32)
    target_slot = (turbine_owner * SLOTS + slot_rank).astype(jnp.int32)
    turbine_grad = jnp.zeros((DEVICES * SLOTS, 2), jnp.float32).at[target_slot].set(grad)
    return (updated, turbine_grad)
```

```python
import math

import jax
import jax.numpy as jnp
from jax import lax
from jax.experimental import pallas as pl
from jax.experimental.pallas import tpu as pltpu
from jax.sharding import PartitionSpec as P

F32 = jnp.float32
BF16 = jnp.bfloat16
NX = 256
NY = 256
SZ = 32
SY = 32
HZ = 16
TURB = 96
STEP = 0.2
VMEM = pl.BlockSpec(memory_space=pltpu.VMEM)
SMEM = pl.BlockSpec(memory_space=pltpu.SMEM)
COST = pl.CostEstimate(flops=1, transcendentals=0, bytes_accessed=1)
PARAMS = pltpu.CompilerParams(vmem_limit_bytes=56 << 20)

DX, YL, YU, YD, ZL, ZH = 0, 1, 2, 3, 4, 5


def split(v):
    hi = v.astype(BF16)
    lo = (v - hi.astype(F32)).astype(BF16)
    return hi, lo


def dot(a, b):
    return lax.dot_general(a, b, (((1,), (0,)), ((), ())), preferred_element_type=F32)


def mix(k_hi, k_lo, v):
    hi, lo = split(v)
    return dot(k_hi, hi) + (dot(k_hi, lo) + dot(k_lo, hi))


def iota(axis):
    return lax.broadcasted_iota(jnp.int32, (256, 256), axis)


def prep_kernel(dx_ref, dy_ref, dz_ref, mats_ref):
    wide, narrow = lax.axis_index("wide"), lax.axis_index("narrow")
    row, col = iota(0), iota(1)
    hi, lo = split(dx_ref[...].T)
    mats_ref[2 * DX] = hi
    mats_ref[2 * DX + 1] = lo
    rows = split(dy_ref[pl.ds(pl.multiple_of(narrow * SY, SY), SY), :])
    spread = (lax.broadcasted_iota(jnp.int32, (256, SY), 0) % SY == lax.broadcasted_iota(jnp.int32, (256, SY), 1)).astype(BF16)
    same = row // SY == col // SY
    for at, shift in ((YL, 0), (YU, -1), (YD, 1)):
        chosen = (row == (narrow + shift) * SY + col % SY).astype(BF16)
        for half in range(2):
            wider = dot(dot(spread, rows[half]).astype(BF16), chosen)
            mats_ref[2 * at + half] = jnp.where(same, wider, 0.0).astype(BF16)
    rows = split(dz_ref[pl.ds(pl.multiple_of(wide * SZ, SZ), SZ), :])
    spread = (lax.broadcasted_iota(jnp.int32, (256, SZ), 0) // 8 == lax.broadcasted_iota(jnp.int32, (256, SZ), 1)).astype(BF16)
    same = row % 8 == col % 8
    source = lax.broadcasted_iota(jnp.int32, (512, 256), 0)
    plane = lax.broadcasted_iota(jnp.int32, (512, 256), 1) // 8
    halo = jnp.where(plane < HZ, plane - HZ, plane - HZ + SZ)
    for at, offset in ((ZL, plane), (ZH, halo)):
        chosen = (source == wide * SZ + offset).astype(BF16)
        for half in range(2):
            wider = dot(dot(spread, rows[half]).astype(BF16), chosen)
            mats_ref[2 * at + half] = jnp.where(same, wider, 0.0).astype(BF16)


def prep(deriv_x, deriv_y, deriv_z):
    return pl.pallas_call(
        prep_kernel,
        in_specs=[VMEM] * 3,
        out_specs=VMEM,
        out_shape=jax.ShapeDtypeStruct((12, 256, 256), BF16),
        compiler_params=PARAMS,
        cost_estimate=COST,
        name="prep",
    )(deriv_x, deriv_y, deriv_z)


def turbine_kernel(block_ref, thrust_ref, owner_ref, ax_ref, ay_ref, ux_ref, weight_ref, force_ref, grad_ref, ax, ay, ux, total, padded, g0, g1):
    wide, narrow = lax.axis_index("wide"), lax.axis_index("narrow")
    cells = SZ * SY
    for half in range(2):
        lanes = pl.ds(128 * half, 128)
        rows = pl.ds(cells * half, cells)
        ax[rows, :] = ax_ref[0, :, :, lanes].reshape(cells, 128)
        ay[rows, :] = ay_ref[0, :, :, lanes].reshape(cells, 128)
        ux[rows, :] = ux_ref[0, :, :, lanes].reshape(cells, 128)
    total[...] = jnp.zeros_like(total)
    padded[...] = jnp.zeros_like(padded)
    g0[...] = jnp.zeros_like(g0)
    g1[...] = jnp.zeros_like(g1)

    def turbine(t, _):
        block = block_ref[0, t]
        start_z = block // (2 * NY) - wide * SZ
        start_y = (block // 2) % NY - narrow * SY
        half = block % 2
        near = (start_z > -SZ) & (start_z < SZ) & (start_y > -2) & (start_y < SY)

        @pl.when(near)
        def _():
            padded[pl.ds(64, 64), :] = weight_ref[t]
            for line in range(2):
                y = start_y + line

                @pl.when((y >= 0) & (y < SY))
                def _():
                    w = padded[pl.ds(64 - 2 * start_z + line, SZ, stride=2), :]
                    rows = pl.ds(half * cells + y, SZ, stride=SY)
                    a, b, u = ax[rows, :], ay[rows, :], ux[rows, :]
                    size = jnp.abs(u)
                    drive = w * (u * size)
                    g0[pl.ds(t, 1), :] += jnp.sum(drive * a, axis=0, keepdims=True)
                    g1[pl.ds(t, 1), :] += jnp.sum(drive * b, axis=0, keepdims=True)
                    total[rows, :] += (thrust_ref[t] * w) * (size * a)

        return 0

    lax.fori_loop(0, TURB, turbine, 0)
    for half in range(2):
        force_ref[:, :, pl.ds(128 * half, 128)] = total[pl.ds(cells * half, cells), :].reshape(SZ, SY, 128)
    ones = jnp.ones((8, 128), F32)
    lanes_sum = lambda g: lax.dot_general(
        ones, g[...], (((1,), (1,)), ((), ())), precision=lax.Precision.HIGHEST, preferred_element_type=F32
    )
    row, col = lax.broadcasted_iota(jnp.int32, (128, 128), 0), lax.broadcasted_iota(jnp.int32, (128, 128), 1)
    owner = owner_ref[0:1, :]
    owner_col = jnp.sum(jnp.where(row == col, owner, 0), axis=1, keepdims=True)
    rank = jnp.sum(((owner_col == owner) & (row < col)).astype(jnp.int32), axis=0, keepdims=True)
    value = jnp.where(row % 2 == 0, lanes_sum(g0)[0:1], lanes_sum(g1)[0:1]) * (1.0 / math.sqrt(128.0 * 64.0))
    value = jnp.where((row < 4) & (rank == row // 2), value, 0.0)
    grad_ref[...] = lax.dot_general(
        (owner == row).astype(F32), value, (((1,), (1,)), ((), ())), precision=lax.Precision.HIGHEST, preferred_element_type=F32
    )


def turbines(rotor_blocks, thrust, owner, adjoint, velocity, weight):
    cells = SZ * SY
    part = lambda c: pl.BlockSpec((1, SZ, SY, NX), lambda i: (c, 0, 0, 0))
    whole = lambda *shape: pl.BlockSpec(shape, lambda i: (0,) * len(shape))
    return pl.pallas_call(
        turbine_kernel,
        grid=(1,),
        in_specs=[SMEM, SMEM, whole(8, 128), part(0), part(1), part(0), whole(TURB, 64, 128)],
        out_specs=[whole(SZ, SY, NX), whole(128, 128)],
        out_shape=[jax.ShapeDtypeStruct((SZ, SY, NX), F32), jax.ShapeDtypeStruct((128, 128), F32)],
        scratch_shapes=[pltpu.VMEM((2 * cells, 128), F32)] * 4 + [pltpu.VMEM((192, 128), F32)] + [pltpu.VMEM((128, 128), F32)] * 2,
        compiler_params=PARAMS,
        cost_estimate=COST,
        name="turbines",
    )(rotor_blocks, thrust, owner, adjoint, adjoint, velocity, weight)


def local_kernel(adj_ref, vel_ref, force_ref, mats_ref, out_ref):
    def lines(yb, _):
        at = pl.ds(pl.multiple_of(yb * 8, 8), 8)
        field = lambda ref, c: ref[c, :, at, :].reshape(256, 256)
        x_hi, x_lo, z_hi, z_lo = mats_ref[2 * DX], mats_ref[2 * DX + 1], mats_ref[2 * ZL], mats_ref[2 * ZL + 1]

        def both(v):
            hi, lo = split(v)
            return (
                dot(hi, x_hi) + (dot(lo, x_hi) + dot(hi, x_lo)),
                dot(z_hi, hi) + (dot(z_hi, lo) + dot(z_lo, hi)),
            )

        stretch_x = jnp.zeros((256, 256), F32)
        stretch_z = jnp.zeros((256, 256), F32)
        for c in range(3):
            dx, dz = both(field(vel_ref, c))
            a = field(adj_ref, c)
            stretch_x += a * dx
            stretch_z += a * dz
        for c in range(3):
            a = field(adj_ref, c)
            dx, dz = both(a)
            tend = field(vel_ref, 0) * dx + field(vel_ref, 2) * dz
            if c == 0:
                tend -= stretch_x + force_ref[:, at, :].reshape(256, 256)
            if c == 2:
                tend -= stretch_z
            out_ref[c, :, at, :] = (a + STEP * tend).reshape(SZ, 8, NX)
        return 0

    lax.fori_loop(0, SY // 8, lines, 0)

    def planes(zg, _):
        at = pl.ds(pl.multiple_of(zg * 8, 8), 8)
        field = lambda ref, c: ref[c, at, :, :].reshape(256, 256)
        y_hi, y_lo = mats_ref[2 * YL], mats_ref[2 * YL + 1]
        stretch = jnp.zeros((256, 256), F32)
        for c in range(3):
            stretch += field(adj_ref, c) * mix(y_hi, y_lo, field(vel_ref, c))
        for c in range(3):
            tend = field(vel_ref, 1) * mix(y_hi, y_lo, field(adj_ref, c))
            if c == 1:
                tend -= stretch
            out_ref[c, at, :, :] = (field(out_ref, c) + STEP * tend).reshape(8, SY, NX)
        return 0

    lax.fori_loop(0, SZ // 8, planes, 0)


def local(adjoint, velocity, force, mats):
    return pl.pallas_call(
        local_kernel,
        in_specs=[VMEM] * 4,
        out_specs=VMEM,
        out_shape=jax.ShapeDtypeStruct(adjoint.shape, F32),
        compiler_params=PARAMS,
        cost_estimate=COST,
        name="local",
    )(adjoint, velocity, force, mats)


def field(ref, c):
    return ref[c].reshape(256, 256)


def adj_kernel(vel_ref, up_ref, down_ref, k_ref, old_ref, out_ref):
    for c in range(3):
        deriv = pair(up_ref, down_ref, c, k_ref)
        out_ref[c] = (field(old_ref, c) + STEP * (field(vel_ref, 0) * deriv)).reshape(out_ref.shape[1:])


def vel_kernel(adj_ref, up_ref, down_ref, k_ref, old_ref, out_ref):
    stretch = jnp.zeros((256, 256), F32)
    for c in range(3):
        stretch += field(adj_ref, c) * pair(up_ref, down_ref, c, k_ref)
    out_ref[0] = (field(old_ref, 0) - STEP * stretch).reshape(out_ref.shape[1:])


def pair(up_ref, down_ref, c, k_ref):
    if k_ref.shape[0] == 2:
        return mix(k_ref[0], k_ref[1], jnp.concatenate([up_ref[c].reshape(128, 256), down_ref[c].reshape(128, 256)], axis=0))
    return mix(k_ref[0], k_ref[1], field(up_ref, c)) + mix(k_ref[2], k_ref[3], field(down_ref, c))


def halo(axis, kind, other, up, down, mats, old):
    at = {"y": 1, "z": 2}[axis]
    n_other, at_other, n_old, at_old = (1, at, 3, 0) if kind == "adj" else (3, 0, 1, at)
    if axis == "y":
        block = lambda n, c: pl.BlockSpec((n, 8, SY, NX), lambda i: (c, i, 0, 0))
        side, mat = block(3, 0), pl.BlockSpec((4, 256, 256), lambda i: (YU // 2, 0, 0))
    else:
        block = lambda n, c: pl.BlockSpec((n, SZ, 8, NX), lambda i: (c, 0, i, 0))
        side, mat = pl.BlockSpec((3, HZ, 8, NX), lambda i: (0, 0, i, 0)), pl.BlockSpec((2, 256, 256), lambda i: (ZH, 0, 0))
    return pl.pallas_call(
        adj_kernel if kind == "adj" else vel_kernel,
        grid=(4,),
        in_specs=[block(n_other, at_other), side, side, mat, block(n_old, at_old)],
        out_specs=block(n_old, at_old),
        out_shape=jax.ShapeDtypeStruct(old.shape, F32),
        input_output_aliases={4: 0},
        compiler_params=PARAMS,
        cost_estimate=COST,
        name=axis + "_" + kind,
    )(other, up, down, mats, old)


def on_device(adjoint, velocity, deriv_x, deriv_y, deriv_z, rotor_blocks, turbine_owner, disk_weight, thrust):
    n_wide, n_narrow = lax.axis_size("wide"), lax.axis_size("narrow")
    up = lambda v, axis, n: lax.ppermute(v, axis, [(i, i + 1) for i in range(n - 1)])
    down = lambda v, axis, n: lax.ppermute(v, axis, [(i + 1, i) for i in range(n - 1)])
    def exchange(v):
        return (
            up(v, "narrow", n_narrow),
            down(v, "narrow", n_narrow),
            up(v[:, HZ:], "wide", n_wide),
            down(v[:, :HZ], "wide", n_wide),
        )

    sides = exchange(adjoint)
    owner = jnp.broadcast_to(jnp.pad(turbine_owner, (0, 128 - TURB), constant_values=-1)[None], (8, 128))
    mats = prep(deriv_x, deriv_y, deriv_z)
    force, grad = turbines(rotor_blocks.T, thrust, owner, adjoint, velocity, disk_weight)
    grad = lax.all_to_all(grad.reshape(n_wide, n_narrow, 128), "wide", split_axis=0, concat_axis=0, tiled=True)
    out = local(adjoint, velocity, force, mats)
    out, grad, velocity, *sides = lax.optimization_barrier((out, grad, velocity, *sides))

    vel_sides = exchange(velocity)
    grad = jnp.sum(grad, axis=0)
    grad = lax.all_to_all(grad.reshape(n_narrow, 1, 128), "narrow", split_axis=0, concat_axis=0, tiled=True)
    out = halo("y", "adj", velocity, sides[0], sides[1], mats, out)
    out = halo("z", "adj", velocity, sides[2], sides[3], mats, out)
    out, grad, *sides = lax.optimization_barrier((out, grad, *vel_sides))

    share = jnp.sum(grad, axis=(0, 1))[:4].reshape(2, 2)
    out = halo("y", "vel", adjoint, sides[0], sides[1], mats, out)
    out = halo("z", "vel", adjoint, sides[2], sides[3], mats, out)
    return out, share


def solution(mesh):
    field = P(None, "wide", "narrow", None)
    return jax.shard_map(
        on_device,
        mesh=mesh,
        in_specs=(field, field) + (P(),) * 7,
        out_specs=(field, P(("wide", "narrow"), None)),
        check_vma=False,
    )
```

```python
import math

import jax
import jax.numpy as jnp
from jax import lax
from jax.experimental import pallas as pl
from jax.experimental.pallas import tpu as pltpu
from jax.sharding import PartitionSpec as P

F32 = jnp.float32
BF16 = jnp.bfloat16
NX = 256
NY = 256
SZ = 32
SY = 32
HZ = 16
TURB = 96
STEP = 0.2
VMEM = pl.BlockSpec(memory_space=pltpu.VMEM)
SMEM = pl.BlockSpec(memory_space=pltpu.SMEM)
HBM = pl.BlockSpec(memory_space=pltpu.HBM)
COST = pl.CostEstimate(flops=1, transcendentals=0, bytes_accessed=1)


def resident(v):
    return pltpu.with_memory_space_constraint(v, pltpu.VMEM)


def call(kernel, operands, outs, name, limit=12, **kw):
    return pl.pallas_call(
        kernel,
        out_shape=outs,
        compiler_params=pltpu.CompilerParams(vmem_limit_bytes=limit << 20),
        cost_estimate=COST,
        name=name,
        **kw,
    )(*operands)


def split(v):
    hi = v.astype(BF16)
    lo = (v - hi.astype(F32)).astype(BF16)
    return hi, lo


def dot(a, b):
    return lax.dot_general(a, b, (((1,), (0,)), ((), ())), preferred_element_type=F32)


def mix(k_hi, k_lo, v):
    hi, lo = split(v)
    return dot(k_hi, hi) + (dot(k_hi, lo) + dot(k_lo, hi))


def iota(axis):
    return lax.broadcasted_iota(jnp.int32, (256, 256), axis)


def prep_kernel(dx_ref, dy_ref, dz_ref, x_ref, z_ref, side_ref, far_ref, near_ref):
    wide, narrow = lax.axis_index("wide"), lax.axis_index("narrow")
    row, col = iota(0), iota(1)
    x_ref[0], x_ref[1] = split(dx_ref[...].T)

    def expand(rows, spread, chosen, same):
        return [jnp.where(same, dot(dot(spread, half).astype(BF16), chosen), 0.0).astype(BF16) for half in rows]

    rows = split(dy_ref[pl.ds(pl.multiple_of(narrow * SY, SY), SY), :])
    spread = (lax.broadcasted_iota(jnp.int32, (256, SY), 0) % SY == lax.broadcasted_iota(jnp.int32, (256, SY), 1)).astype(BF16)
    odd = narrow % 2
    other = narrow + 2 * odd - 1
    partner = narrow + 1 - 2 * odd
    chosen = (row == other * SY + col % SY).astype(BF16)
    far_ref[0], far_ref[1] = expand(rows, spread, chosen, row // SY == col // SY)
    chosen = (row == jnp.where((col // SY) % 2 == 0, narrow, partner) * SY + col % SY).astype(BF16)
    near_ref[0], near_ref[1] = expand(rows, spread[:128], chosen, row[:128] // SY == col[:128] // (2 * SY))
    rows = split(dz_ref[pl.ds(pl.multiple_of(wide * SZ, SZ), SZ), :])
    spread = (lax.broadcasted_iota(jnp.int32, (256, SZ), 0) // 8 == lax.broadcasted_iota(jnp.int32, (256, SZ), 1)).astype(BF16)
    source = lax.broadcasted_iota(jnp.int32, (512, 256), 0)
    plane = lax.broadcasted_iota(jnp.int32, (512, 256), 1) // 8
    halo = jnp.where(plane < HZ, plane - HZ, plane - HZ + SZ)
    for out_ref, offset in ((z_ref, plane), (side_ref, halo)):
        chosen = (source == wide * SZ + offset).astype(BF16)
        out_ref[0], out_ref[1] = expand(rows, spread, chosen, row % 8 == col % 8)


def prep(deriv_x, deriv_y, deriv_z):
    outs = [pltpu.VMEM((2, rows, 256), BF16) for rows in (256, 256, 256, 256, 128)]
    return call(prep_kernel, (deriv_x, deriv_y, deriv_z), outs, "prep", in_specs=[VMEM] * 3, out_specs=[VMEM] * 5)


def turbine_kernel(block_ref, thrust_ref, owner_ref, adj_ref, vel_ref, weight_ref, force_ref, grad_ref, ax, ay, ux, total, padded, g0, g1):
    wide, narrow = lax.axis_index("wide"), lax.axis_index("narrow")
    cells = SZ * SY
    for half in range(2):
        lanes = pl.ds(128 * half, 128)
        rows = pl.ds(cells * half, cells)
        ax[rows, :] = adj_ref[0, :, :, lanes].reshape(cells, 128)
        ay[rows, :] = adj_ref[1, :, :, lanes].reshape(cells, 128)
        ux[rows, :] = vel_ref[0, :, :, lanes].reshape(cells, 128)
    total[...] = jnp.zeros_like(total)
    padded[...] = jnp.zeros_like(padded)
    g0[...] = jnp.zeros_like(g0)
    g1[...] = jnp.zeros_like(g1)

    def turbine(t, _):
        block = block_ref[0, t]
        start_z = block // (2 * NY) - wide * SZ
        start_y = (block // 2) % NY - narrow * SY
        half = block % 2
        near = (start_z > -SZ) & (start_z < SZ) & (start_y > -2) & (start_y < SY)

        @pl.when(near)
        def _():
            padded[pl.ds(64, 64), :] = weight_ref[t]
            for line in range(2):
                y = start_y + line

                @pl.when((y >= 0) & (y < SY))
                def _():
                    w = padded[pl.ds(64 - 2 * start_z + line, SZ, stride=2), :]
                    rows = pl.ds(half * cells + y, SZ, stride=SY)
                    a, b, u = ax[rows, :], ay[rows, :], ux[rows, :]
                    size = jnp.abs(u)
                    drive = w * (u * size)
                    g0[pl.ds(t, 1), :] += jnp.sum(drive * a, axis=0, keepdims=True)
                    g1[pl.ds(t, 1), :] += jnp.sum(drive * b, axis=0, keepdims=True)
                    total[rows, :] += (thrust_ref[t] * w) * (size * a)

        return 0

    lax.fori_loop(0, TURB, turbine, 0)
    for half in range(2):
        force_ref[:, :, pl.ds(128 * half, 128)] = total[pl.ds(cells * half, cells), :].reshape(SZ, SY, 128)
    ones = jnp.ones((8, 128), F32)
    lanes_sum = lambda g: lax.dot_general(
        ones, g[...], (((1,), (1,)), ((), ())), precision=lax.Precision.HIGHEST, preferred_element_type=F32
    )
    row, col = lax.broadcasted_iota(jnp.int32, (128, 128), 0), lax.broadcasted_iota(jnp.int32, (128, 128), 1)
    owner = owner_ref[0:1, :]
    owner_col = jnp.sum(jnp.where(row == col, owner, 0), axis=1, keepdims=True)
    rank = jnp.sum(((owner_col == owner) & (row < col)).astype(jnp.int32), axis=0, keepdims=True)
    value = jnp.where(row % 2 == 0, lanes_sum(g0)[0:1], lanes_sum(g1)[0:1]) * (1.0 / math.sqrt(128.0 * 64.0))
    value = jnp.where((row < 4) & (rank == row // 2), value, 0.0)
    grad_ref[...] = lax.dot_general(
        (owner == row).astype(F32), value, (((1,), (1,)), ((), ())), precision=lax.Precision.HIGHEST, preferred_element_type=F32
    )


def turbines(blocks, thrust, owner, adjoint, velocity, weight):
    scratch = [pltpu.VMEM((2 * SZ * SY, 128), F32)] * 4 + [pltpu.VMEM((192, 128), F32)] + [pltpu.VMEM((128, 128), F32)] * 2
    outs = [pltpu.VMEM((SZ, SY, NX), F32), jax.ShapeDtypeStruct((128, 128), F32)]
    operands = (blocks, thrust, owner, adjoint, velocity, weight)
    return call(turbine_kernel, operands, outs, "turbines", 16, in_specs=[SMEM] * 2 + [VMEM] * 4, out_specs=[VMEM] * 2, scratch_shapes=scratch)


def copy_of(source, target, sem):
    return pltpu.make_async_copy(source, target, sem)


def chip_lines(one, two, c, at):
    return jnp.stack([one[c, at, :, :], two[c, at, :, :]], axis=1).reshape(256, 256)


def xz_kernel(adj_ref, vel_ref, force_ref, x_ref, z_ref, out_ref, tend, sems):
    stores = []
    for yb in range(SY // 8):
        at = pl.ds(yb * 8, 8)
        field = lambda ref, c: ref[c, :, at, :].reshape(256, 256)
        x_hi, x_lo, z_hi, z_lo = x_ref[0], x_ref[1], z_ref[0], z_ref[1]

        def both(v):
            hi, lo = split(v)
            return (
                dot(hi, x_hi) + (dot(lo, x_hi) + dot(hi, x_lo)),
                dot(z_hi, hi) + (dot(z_hi, lo) + dot(z_lo, hi)),
            )

        stretch_x = jnp.zeros((256, 256), F32)
        stretch_z = jnp.zeros((256, 256), F32)
        for c in range(3):
            dx, dz = both(field(vel_ref, c))
            a = field(adj_ref, c)
            stretch_x += a * dx
            stretch_z += a * dz
        for c in range(3):
            a = field(adj_ref, c)
            dx, dz = both(a)
            total = field(vel_ref, 0) * dx + field(vel_ref, 2) * dz
            if c == 0:
                total -= stretch_x + force_ref[:, at, :].reshape(256, 256)
            if c == 2:
                total -= stretch_z
            tend[c, :, at, :] = (a + STEP * total).reshape(SZ, 8, NX)
        stores.append(copy_of(tend.at[:, :, at], out_ref.at[:, :, at], sems.at[yb]))
        stores[-1].start()
    for copy in stores:
        copy.wait()


def side_lines(up_ref, down_ref, c, at):
    return jnp.concatenate([up_ref[c, :, at, :].reshape(128, 256), down_ref[c, :, at, :].reshape(128, 256)], axis=0)


def adj_kernel(vel_ref, far_ref, up_ref, down_ref, y_ref, z_ref, old_ref, out_ref):
    def planes(g, _):
        at = pl.ds(pl.multiple_of(g * 8, 8), 8)
        field = lambda ref, c: ref[c, at, :, :].reshape(256, 256)
        for c in range(3):
            total = field(vel_ref, 1) * mix(y_ref[0], y_ref[1], field(far_ref, c))
            out_ref[c, at, :, :] = (field(old_ref, c) + STEP * total).reshape(8, SY, NX)
        return 0

    def lines(yb, _):
        at = pl.ds(pl.multiple_of(yb * 8, 8), 8)
        field = lambda ref, c: ref[c, :, at, :].reshape(256, 256)
        for c in range(3):
            total = field(vel_ref, 2) * mix(z_ref[0], z_ref[1], side_lines(up_ref, down_ref, c, at))
            out_ref[c, :, at, :] = (field(out_ref, c) + STEP * total).reshape(SZ, 8, NX)
        return 0

    lax.fori_loop(0, SZ // 8, planes, 0)
    lax.fori_loop(0, SY // 8, lines, 0)


def near_kernel(adj_ref, vel_ref, adj2_ref, vel2_ref, k_ref, old_ref, done_ref, rest_ref, stage, sem):
    def planes(g, _):
        at = pl.ds(pl.multiple_of(g * 4, 4), 4)
        field = lambda ref, c: ref[c, at, :, :].reshape(128, 256)
        both = jnp.concatenate([k_ref[0], k_ref[1]], axis=0)

        def deriv(one, two, c):
            hi, lo = split(chip_lines(one, two, c, at))
            most = dot(both, hi)
            return most[:128] + (most[128:] + dot(k_ref[0], lo))

        stretch = jnp.zeros((128, 256), F32)
        for c in range(3):
            stretch += field(adj_ref, c) * deriv(vel_ref, vel2_ref, c)
        for c in range(3):
            total = field(vel_ref, 1) * deriv(adj_ref, adj2_ref, c)
            if c == 1:
                total -= stretch
            total = (field(old_ref, c) + STEP * total).reshape(4, SY, NX)
            if c == 0:
                stage[at, :, :] = total
            else:
                rest_ref[c - 1, at, :, :] = total
        return 0

    lax.fori_loop(0, SZ // 4, planes, 0)
    store = copy_of(stage, done_ref.at[0], sem)
    store.start()
    store.wait()


def vel_kernel(adj_ref, far_ref, up_ref, down_ref, y_ref, z_ref, rest_ref, done_ref, out_ref, token_ref, stage, sems):
    del done_ref
    token_ref[...] = jnp.zeros_like(token_ref)
    stores = []
    for g in range(SZ // 8):
        at = pl.ds(8 * g, 8)
        field = lambda ref, c: ref[c, at, :, :].reshape(256, 256)
        stretch = jnp.zeros((256, 256), F32)
        for c in range(3):
            stretch += field(adj_ref, c) * mix(y_ref[0], y_ref[1], field(far_ref, c))
        stage[0, at, :, :] = (field(rest_ref, 0) - STEP * stretch).reshape(8, SY, NX)
        stores.append(copy_of(stage.at[0, at], out_ref.at[1, at], sems.at[0, g]))
        stores[-1].start()
    for yb in range(SY // 8):
        at = pl.ds(8 * yb, 8)
        field = lambda ref, c: ref[c, :, at, :].reshape(256, 256)
        stretch = jnp.zeros((256, 256), F32)
        for c in range(3):
            stretch += field(adj_ref, c) * mix(z_ref[0], z_ref[1], side_lines(up_ref, down_ref, c, at))
        stage[1, :, at, :] = (field(rest_ref, 1) - STEP * stretch).reshape(SZ, 8, NX)
        stores.append(copy_of(stage.at[1, :, at], out_ref.at[2, :, at], sems.at[1, yb]))
        stores[-1].start()
    for copy in stores:
        copy.wait()


def share_kernel(terms_ref, done_ref, out_ref):
    del done_ref
    total = jnp.sum(terms_ref[...].reshape(128, 128), axis=0, keepdims=True)
    out_ref[0:1, :] = total[:, 0:2]
    out_ref[1:2, :] = total[:, 2:4]


def on_device(adjoint, velocity, deriv_x, deriv_y, deriv_z, rotor_blocks, turbine_owner, disk_weight, thrust):
    n_wide, n_narrow = lax.axis_size("wide"), lax.axis_size("narrow")
    up = [(i, i + 1) for i in range(n_wide - 1)]
    down = [(i + 1, i) for i in range(n_wide - 1)]
    chip = [(i, i ^ 1) for i in range(n_narrow)]
    across = [pair for i in range(1, n_narrow - 1, 2) for pair in ((i, i + 1), (i + 1, i))]
    barrier = lax.optimization_barrier
    shape = jax.ShapeDtypeStruct(adjoint.shape, F32)
    field = pltpu.VMEM(adjoint.shape, F32)
    dma = pltpu.SemaphoreType.DMA

    def exchange(v, upper, lower):
        return lax.ppermute(v, "narrow", across), lax.ppermute(upper, "wide", up), lax.ppermute(lower, "wide", down)

    first, upper, lower = barrier((adjoint, adjoint[:, HZ:], adjoint[:, :HZ]))
    sides = exchange(first, upper, lower)
    adj, vel = resident(adjoint), resident(velocity)
    owner = jnp.broadcast_to(jnp.pad(turbine_owner, (0, 128 - TURB), constant_values=-1)[None], (8, 128))
    force, grad = turbines(rotor_blocks.T, thrust, owner, adj, vel, resident(disk_weight))
    grad = lax.all_to_all(grad.reshape(n_wide * n_narrow, 1, 128), ("wide", "narrow"), split_axis=0, concat_axis=0, tiled=True)
    m_x, m_z, m_side, m_far, m_near = prep(deriv_x, deriv_y, deriv_z)
    out = call(
        xz_kernel, (adj, vel, force, m_x, m_z), shape, "xz", 16, in_specs=[VMEM] * 5, out_specs=HBM, scratch_shapes=[field, dma((4,))]
    )
    out, grad, adjoint, velocity, upper, lower, *sides = barrier(
        (out, grad, adjoint, velocity, velocity[:, HZ:], velocity[:, :HZ], *sides)
    )

    vel_sides = exchange(velocity, upper, lower)
    near = [resident(lax.ppermute(v, "narrow", chip)) for v in (adjoint, velocity)]
    adj, vel = resident(adjoint), resident(velocity)
    operands = (vel, *[resident(v) for v in sides], m_far, m_side, resident(out))
    out = call(adj_kernel, operands, field, "halo_adj", in_specs=[VMEM] * 7, out_specs=VMEM)
    out, rest = call(
        near_kernel,
        (adj, vel, *near, m_near, out),
        [shape, pltpu.VMEM((2, SZ, SY, NX), F32)],
        "near",
        in_specs=[VMEM] * 6,
        out_specs=[HBM, VMEM],
        scratch_shapes=[pltpu.VMEM((SZ, SY, NX), F32), dma(())],
    )
    out, token = call(
        vel_kernel,
        (adj, *[resident(v) for v in vel_sides], m_far, m_side, rest, out),
        [shape, jax.ShapeDtypeStruct((8, 128), F32)],
        "halo_vel",
        in_specs=[VMEM] * 7 + [HBM],
        out_specs=[HBM, VMEM],
        input_output_aliases={7: 0},
        scratch_shapes=[pltpu.VMEM((2, SZ, SY, NX), F32), dma((2, 4))],
    )
    share = call(share_kernel, (grad, token), jax.ShapeDtypeStruct((2, 2), F32), "share", in_specs=[VMEM] * 2, out_specs=VMEM)
    return out, share


def solution(mesh):
    field = P(None, "wide", "narrow", None)
    return jax.shard_map(
        on_device,
        mesh=mesh,
        in_specs=(field, field) + (P(),) * 7,
        out_specs=(field, P(("wide", "narrow"), None)),
        check_vma=False,
    )
```

```python
import math

import jax
import jax.numpy as jnp
from jax import lax
from jax.experimental import pallas as pl
from jax.experimental.pallas import tpu as pltpu
from jax.sharding import PartitionSpec as P

F32 = jnp.float32
BF16 = jnp.bfloat16
NX = 256
NY = 256
SZ = 32
SY = 32
HZ = 16
TURB = 96
STEP = 0.2
VMEM = pl.BlockSpec(memory_space=pltpu.VMEM)
SMEM = pl.BlockSpec(memory_space=pltpu.SMEM)
HBM = pl.BlockSpec(memory_space=pl.ANY)
COST = pl.CostEstimate(flops=1, transcendentals=0, bytes_accessed=1)


def resident(v):
    return pltpu.with_memory_space_constraint(v, pltpu.VMEM)


def call(kernel, operands, outs, name, limit=12, **kw):
    return pl.pallas_call(
        kernel,
        out_shape=outs,
        compiler_params=pltpu.CompilerParams(vmem_limit_bytes=limit << 20),
        cost_estimate=COST,
        name=name,
        **kw,
    )(*operands)


def split(v):
    hi = v.astype(BF16)
    lo = (v - hi.astype(F32)).astype(BF16)
    return hi, lo


def dot(a, b):
    return lax.dot_general(a, b, (((1,), (0,)), ((), ())), preferred_element_type=F32)


def mix(k_hi, k_lo, v):
    hi, lo = split(v)
    return dot(k_hi, hi) + (dot(k_hi, lo) + dot(k_lo, hi))


def iota(axis):
    return lax.broadcasted_iota(jnp.int32, (256, 256), axis)


def prep_kernel(dx_ref, dy_ref, dz_ref, x_ref, z_ref, side_ref, far_ref, near_ref, token_ref):
    token_ref[...] = jnp.zeros_like(token_ref)
    wide, narrow = lax.axis_index("wide"), lax.axis_index("narrow")
    row, col = iota(0), iota(1)
    x_ref[0], x_ref[1] = split(dx_ref[...].T)

    def expand(rows, spread, chosen, same):
        return [jnp.where(same, dot(dot(spread, half).astype(BF16), chosen), 0.0).astype(BF16) for half in rows]

    rows = split(dy_ref[pl.ds(pl.multiple_of(narrow * SY, SY), SY), :])
    spread = (lax.broadcasted_iota(jnp.int32, (256, SY), 0) % SY == lax.broadcasted_iota(jnp.int32, (256, SY), 1)).astype(BF16)
    odd = narrow % 2
    other = narrow + 2 * odd - 1
    partner = narrow + 1 - 2 * odd
    chosen = (row == other * SY + col % SY).astype(BF16)
    far_ref[0], far_ref[1] = expand(rows, spread, chosen, row // SY == col // SY)
    chosen = (row == jnp.where((col // SY) % 2 == 0, narrow, partner) * SY + col % SY).astype(BF16)
    near_ref[0], near_ref[1] = expand(rows, spread[:128], chosen, row[:128] // SY == col[:128] // (2 * SY))
    rows = split(dz_ref[pl.ds(pl.multiple_of(wide * SZ, SZ), SZ), :])
    spread = (lax.broadcasted_iota(jnp.int32, (256, SZ), 0) // 8 == lax.broadcasted_iota(jnp.int32, (256, SZ), 1)).astype(BF16)
    source = lax.broadcasted_iota(jnp.int32, (512, 256), 0)
    plane = lax.broadcasted_iota(jnp.int32, (512, 256), 1) // 8
    halo = jnp.where(plane < HZ, plane - HZ, plane - HZ + SZ)
    for out_ref, offset in ((z_ref, plane), (side_ref, halo)):
        chosen = (source == wide * SZ + offset).astype(BF16)
        out_ref[0], out_ref[1] = expand(rows, spread, chosen, row % 8 == col % 8)


def prep(deriv_x, deriv_y, deriv_z):
    outs = [pltpu.VMEM((2, rows, 256), BF16) for rows in (256, 256, 256, 256, 128)]
    outs.append(jax.ShapeDtypeStruct((8, 128), F32))
    return call(prep_kernel, (deriv_x, deriv_y, deriv_z), outs, "prep", in_specs=[VMEM] * 3, out_specs=[VMEM] * 6)


def turbine_kernel(block_ref, thrust_ref, owner_ref, adj_ref, vel_ref, weight_ref, force_ref, grad_ref, ax, ay, ux, total, padded, g0, g1):
    wide, narrow = lax.axis_index("wide"), lax.axis_index("narrow")
    cells = SZ * SY
    for half in range(2):
        lanes = pl.ds(128 * half, 128)
        rows = pl.ds(cells * half, cells)
        ax[rows, :] = adj_ref[0, :, :, lanes].reshape(cells, 128)
        ay[rows, :] = adj_ref[1, :, :, lanes].reshape(cells, 128)
        ux[rows, :] = vel_ref[0, :, :, lanes].reshape(cells, 128)
    total[...] = jnp.zeros_like(total)
    padded[...] = jnp.zeros_like(padded)
    g0[...] = jnp.zeros_like(g0)
    g1[...] = jnp.zeros_like(g1)

    def turbine(t, _):
        block = block_ref[0, t]
        start_z = block // (2 * NY) - wide * SZ
        start_y = (block // 2) % NY - narrow * SY
        half = block % 2
        near = (start_z > -SZ) & (start_z < SZ) & (start_y > -2) & (start_y < SY)

        @pl.when(near)
        def _():
            padded[pl.ds(64, 64), :] = weight_ref[t]
            for line in range(2):
                y = start_y + line

                @pl.when((y >= 0) & (y < SY))
                def _():
                    w = padded[pl.ds(64 - 2 * start_z + line, SZ, stride=2), :]
                    rows = pl.ds(half * cells + y, SZ, stride=SY)
                    a, b, u = ax[rows, :], ay[rows, :], ux[rows, :]
                    size = jnp.abs(u)
                    drive = w * (u * size)
                    g0[pl.ds(t, 1), :] += jnp.sum(drive * a, axis=0, keepdims=True)
                    g1[pl.ds(t, 1), :] += jnp.sum(drive * b, axis=0, keepdims=True)
                    total[rows, :] += (thrust_ref[t] * w) * (size * a)

        return 0

    lax.fori_loop(0, TURB, turbine, 0)
    for half in range(2):
        force_ref[:, :, pl.ds(128 * half, 128)] = total[pl.ds(cells * half, cells), :].reshape(SZ, SY, 128)
    ones = jnp.ones((8, 128), F32)
    lanes_sum = lambda g: lax.dot_general(
        ones, g[...], (((1,), (1,)), ((), ())), precision=lax.Precision.HIGHEST, preferred_element_type=F32
    )
    row, col = lax.broadcasted_iota(jnp.int32, (128, 128), 0), lax.broadcasted_iota(jnp.int32, (128, 128), 1)
    owner = owner_ref[0:1, :]
    owner_col = jnp.sum(jnp.where(row == col, owner, 0), axis=1, keepdims=True)
    rank = jnp.sum(((owner_col == owner) & (row < col)).astype(jnp.int32), axis=0, keepdims=True)
    value = jnp.where(row % 2 == 0, lanes_sum(g0)[0:1], lanes_sum(g1)[0:1]) * (1.0 / math.sqrt(128.0 * 64.0))
    value = jnp.where((row < 4) & (rank == row // 2), value, 0.0)
    grad_ref[...] = lax.dot_general(
        (owner == row).astype(F32), value, (((1,), (1,)), ((), ())), precision=lax.Precision.HIGHEST, preferred_element_type=F32
    )


def turbines(blocks, thrust, owner, adjoint, velocity, weight):
    scratch = [pltpu.VMEM((2 * SZ * SY, 128), F32)] * 4 + [pltpu.VMEM((192, 128), F32)] + [pltpu.VMEM((128, 128), F32)] * 2
    outs = [pltpu.VMEM((SZ, SY, NX), F32), jax.ShapeDtypeStruct((128, 128), F32)]
    operands = (blocks, thrust, owner, adjoint, velocity, weight)
    return call(turbine_kernel, operands, outs, "turbines", 16, in_specs=[SMEM] * 2 + [VMEM] * 4, out_specs=[VMEM] * 2, scratch_shapes=scratch)


def copy_of(source, target, sem):
    return pltpu.make_async_copy(source, target, sem)


def chip_lines(one, two, c, at):
    return jnp.stack([one[c, at, :, :], two[c, at, :, :]], axis=1).reshape(256, 256)


def xz_kernel(token_ref, adj_ref, vel_ref, force_ref, x_ref, z_ref, out_ref, next_ref, tend, sems):
    next_ref[...] = token_ref[...]
    stores = []
    for yb in range(SY // 8):
        at = pl.ds(yb * 8, 8)
        field = lambda ref, c: ref[c, :, at, :].reshape(256, 256)
        x_hi, x_lo, z_hi, z_lo = x_ref[0], x_ref[1], z_ref[0], z_ref[1]

        def both(v):
            hi, lo = split(v)
            return (
                dot(hi, x_hi) + (dot(lo, x_hi) + dot(hi, x_lo)),
                dot(z_hi, hi) + (dot(z_hi, lo) + dot(z_lo, hi)),
            )

        stretch_x = jnp.zeros((256, 256), F32)
        stretch_z = jnp.zeros((256, 256), F32)
        for c in range(3):
            dx, dz = both(field(vel_ref, c))
            a = field(adj_ref, c)
            stretch_x += a * dx
            stretch_z += a * dz
        for c in range(3):
            a = field(adj_ref, c)
            dx, dz = both(a)
            total = field(vel_ref, 0) * dx + field(vel_ref, 2) * dz
            if c == 0:
                total -= stretch_x + force_ref[:, at, :].reshape(256, 256)
            if c == 2:
                total -= stretch_z
            tend[c, :, at, :] = (a + STEP * total).reshape(SZ, 8, NX)
        stores.append(copy_of(tend.at[:, :, at], out_ref.at[:, :, at], sems.at[yb]))
        stores[-1].start()
    for copy in stores:
        copy.wait()


def side_lines(up_ref, down_ref, c, at):
    return jnp.concatenate([up_ref[c, :, at, :].reshape(128, 256), down_ref[c, :, at, :].reshape(128, 256)], axis=0)


def adj_kernel(vel_ref, far_ref, up_ref, down_ref, y_ref, z_ref, old_ref, out_ref):
    def planes(g, _):
        at = pl.ds(pl.multiple_of(g * 8, 8), 8)
        field = lambda ref, c: ref[c, at, :, :].reshape(256, 256)
        for c in range(3):
            total = field(vel_ref, 1) * mix(y_ref[0], y_ref[1], field(far_ref, c))
            out_ref[c, at, :, :] = (field(old_ref, c) + STEP * total).reshape(8, SY, NX)
        return 0

    def lines(yb, _):
        at = pl.ds(pl.multiple_of(yb * 8, 8), 8)
        field = lambda ref, c: ref[c, :, at, :].reshape(256, 256)
        for c in range(3):
            total = field(vel_ref, 2) * mix(z_ref[0], z_ref[1], side_lines(up_ref, down_ref, c, at))
            out_ref[c, :, at, :] = (field(out_ref, c) + STEP * total).reshape(SZ, 8, NX)
        return 0

    lax.fori_loop(0, SZ // 8, planes, 0)
    lax.fori_loop(0, SY // 8, lines, 0)


def near_kernel(before_ref, adj_ref, vel_ref, adj2_ref, vel2_ref, k_ref, old_ref, done_ref, rest_ref, token_ref, stage, sem):
    token_ref[...] = before_ref[...]

    def planes(g, _):
        at = pl.ds(pl.multiple_of(g * 4, 4), 4)
        field = lambda ref, c: ref[c, at, :, :].reshape(128, 256)
        both = jnp.concatenate([k_ref[0], k_ref[1]], axis=0)

        def deriv(one, two, c):
            hi, lo = split(chip_lines(one, two, c, at))
            most = dot(both, hi)
            return most[:128] + (most[128:] + dot(k_ref[0], lo))

        stretch = jnp.zeros((128, 256), F32)
        for c in range(3):
            stretch += field(adj_ref, c) * deriv(vel_ref, vel2_ref, c)
        for c in range(3):
            total = field(vel_ref, 1) * deriv(adj_ref, adj2_ref, c)
            if c == 1:
                total -= stretch
            total = (field(old_ref, c) + STEP * total).reshape(4, SY, NX)
            if c == 0:
                stage[at, :, :] = total
            else:
                rest_ref[c - 1, at, :, :] = total
        return 0

    lax.fori_loop(0, SZ // 4, planes, 0)
    store = copy_of(stage, done_ref.at[0], sem)
    store.start()
    store.wait()


def far_kernel(token_ref, adj_ref, far_ref, k_ref, rest_ref, done_ref, out_ref, last_ref, stage, sems):
    del token_ref, done_ref
    stores = []
    for g in range(SZ // 8):
        at = pl.ds(8 * g, 8)
        field = lambda ref, c: ref[c, at, :, :].reshape(256, 256)
        stretch = jnp.zeros((256, 256), F32)
        for c in range(3):
            stretch += field(adj_ref, c) * mix(k_ref[0], k_ref[1], field(far_ref, c))
        stage[at, :, :] = (field(rest_ref, 0) - STEP * stretch).reshape(8, SY, NX)
        stores.append(copy_of(stage.at[at], out_ref.at[1, at], sems.at[g]))
        stores[-1].start()
    last_ref[...] = rest_ref[1]
    for copy in stores:
        copy.wait()


def z_kernel(adj_ref, up_ref, down_ref, k_ref, last_ref, done_ref, out_ref, token_ref, stage, sems):
    del done_ref
    token_ref[...] = jnp.zeros_like(token_ref)
    stores = []
    for yb in range(SY // 8):
        at = pl.ds(8 * yb, 8)
        field = lambda ref, c: ref[c, :, at, :].reshape(256, 256)
        stretch = jnp.zeros((256, 256), F32)
        for c in range(3):
            stretch += field(adj_ref, c) * mix(k_ref[0], k_ref[1], side_lines(up_ref, down_ref, c, at))
        stage[:, at, :] = (last_ref[:, at, :].reshape(256, 256) - STEP * stretch).reshape(SZ, 8, NX)
        stores.append(copy_of(stage.at[:, at], out_ref.at[2, :, at], sems.at[yb]))
        stores[-1].start()
    for copy in stores:
        copy.wait()


def share_kernel(terms_ref, done_ref, out_ref):
    del done_ref
    total = jnp.sum(terms_ref[...].reshape(128, 128), axis=0, keepdims=True)
    out_ref[0:1, :] = total[:, 0:2]
    out_ref[1:2, :] = total[:, 2:4]


def on_device(adjoint, velocity, deriv_x, deriv_y, deriv_z, rotor_blocks, turbine_owner, disk_weight, thrust):
    n_wide, n_narrow = lax.axis_size("wide"), lax.axis_size("narrow")
    up = [(i, i + 1) for i in range(n_wide - 1)]
    down = [(i + 1, i) for i in range(n_wide - 1)]
    chip = [(i, i ^ 1) for i in range(n_narrow)]
    across = [pair for i in range(1, n_narrow - 1, 2) for pair in ((i, i + 1), (i + 1, i))]
    barrier = lax.optimization_barrier
    shape = jax.ShapeDtypeStruct(adjoint.shape, F32)
    field = pltpu.VMEM(adjoint.shape, F32)
    dma = pltpu.SemaphoreType.DMA

    small = jax.ShapeDtypeStruct((8, 128), F32)
    far = lambda v: lax.ppermute(v, "narrow", across)
    sides = lambda upper, lower: [lax.ppermute(upper, "wide", up), lax.ppermute(lower, "wide", down)]

    first, upper, lower = barrier((adjoint, adjoint[:, HZ:], adjoint[:, :HZ]))
    adj_sides = sides(upper, lower)
    adj_far = far(first)
    near = [lax.ppermute(v, "narrow", chip) for v in (first, velocity)]
    adj, vel = resident(adjoint), resident(velocity)
    owner = jnp.broadcast_to(jnp.pad(turbine_owner, (0, 128 - TURB), constant_values=-1)[None], (8, 128))
    force, grad = turbines(rotor_blocks.T, thrust, owner, adj, vel, resident(disk_weight))
    deriv_y, grad, *near = barrier((deriv_y, grad, *near))
    m_x, m_z, m_side, m_far, m_near, token = prep(deriv_x, deriv_y, deriv_z)
    grad = lax.all_to_all(grad.reshape(n_wide * n_narrow, 1, 128), ("wide", "narrow"), split_axis=0, concat_axis=0, tiled=True)
    out, token = call(
        xz_kernel,
        (token, adj, vel, force, m_x, m_z),
        [shape, small],
        "xz",
        16,
        in_specs=[VMEM] * 6,
        out_specs=[HBM, VMEM],
        scratch_shapes=[field, dma((4,))],
    )
    token, gated = barrier((token, velocity))
    vel_far = far(gated)
    out, upper, lower, adj_far, *adj_sides = barrier(
        (out, velocity[:, HZ:], velocity[:, :HZ], adj_far, *adj_sides)
    )

    vel_sides = sides(upper, lower)
    adj, vel = resident(adjoint), resident(velocity)
    operands = (vel, *[resident(v) for v in (adj_far, *adj_sides)], m_far, m_side, resident(out))
    out = call(adj_kernel, operands, field, "halo_adj", in_specs=[VMEM] * 7, out_specs=VMEM)
    out, rest, token = call(
        near_kernel,
        (token, adj, vel, *[resident(v) for v in near], m_near, out),
        [shape, pltpu.VMEM((2, SZ, SY, NX), F32), small],
        "near",
        in_specs=[VMEM] * 7,
        out_specs=[HBM, VMEM, VMEM],
        scratch_shapes=[pltpu.VMEM((SZ, SY, NX), F32), dma(())],
    )
    token, vel_far = barrier((token, vel_far))
    plane = pltpu.VMEM((SZ, SY, NX), F32)
    out, last = call(
        far_kernel,
        (token, adj, resident(vel_far), m_far, rest, out),
        [shape, plane],
        "far_vel",
        in_specs=[VMEM] * 5 + [HBM],
        out_specs=[HBM, VMEM],
        input_output_aliases={5: 0},
        scratch_shapes=[plane, dma((4,))],
    )
    out, token = call(
        z_kernel,
        (adj, *[resident(v) for v in vel_sides], m_side, last, out),
        [shape, small],
        "z_vel",
        in_specs=[VMEM] * 5 + [HBM],
        out_specs=[HBM, VMEM],
        input_output_aliases={5: 0},
        scratch_shapes=[plane, dma((4,))],
    )
    share = call(share_kernel, (grad, token), jax.ShapeDtypeStruct((2, 2), F32), "share", in_specs=[VMEM] * 2, out_specs=VMEM)
    return out, share


def solution(mesh):
    field = P(None, "wide", "narrow", None)
    return jax.shard_map(
        on_device,
        mesh=mesh,
        in_specs=(field, field) + (P(),) * 7,
        out_specs=(field, P(("wide", "narrow"), None)),
        check_vma=False,
    )
```

```python
import math

import jax
import jax.numpy as jnp
from jax import lax
from jax.experimental import pallas as pl
from jax.experimental.pallas import tpu as pltpu
from jax.sharding import PartitionSpec as P

F32 = jnp.float32
BF16 = jnp.bfloat16
NX = 256
NY = 256
SZ = 32
SY = 32
HZ = 16
TURB = 96
STEP = 0.2
VMEM = pl.BlockSpec(memory_space=pltpu.VMEM)
SMEM = pl.BlockSpec(memory_space=pltpu.SMEM)
HBM = pl.BlockSpec(memory_space=pl.ANY)
COST = pl.CostEstimate(flops=1, transcendentals=0, bytes_accessed=1)


def resident(v):
    return pltpu.with_memory_space_constraint(v, pltpu.VMEM)


def in_hbm(v):
    return pltpu.with_memory_space_constraint(v, pltpu.HBM)


def call(kernel, operands, outs, name, limit=12, **kw):
    return pl.pallas_call(
        kernel,
        out_shape=outs,
        compiler_params=pltpu.CompilerParams(vmem_limit_bytes=limit << 20),
        cost_estimate=COST,
        name=name,
        **kw,
    )(*operands)


def split(v):
    hi = v.astype(BF16)
    lo = (v - hi.astype(F32)).astype(BF16)
    return hi, lo


def dot(a, b):
    return lax.dot_general(a, b, (((1,), (0,)), ((), ())), preferred_element_type=F32)


def mix(k_hi, k_lo, v):
    hi, lo = split(v)
    return dot(k_hi, hi) + (dot(k_hi, lo) + dot(k_lo, hi))


def iota(axis):
    return lax.broadcasted_iota(jnp.int32, (256, 256), axis)


def prep_kernel(dx_ref, dy_ref, dz_ref, x_ref, z_ref, side_ref, far_ref, near_ref, token_ref):
    token_ref[...] = jnp.zeros_like(token_ref)
    wide, narrow = lax.axis_index("wide"), lax.axis_index("narrow")
    row, col = iota(0), iota(1)
    x_ref[0], x_ref[1] = split(dx_ref[...].T)

    def expand(rows, spread, chosen, same):
        return [jnp.where(same, dot(dot(spread, half).astype(BF16), chosen), 0.0).astype(BF16) for half in rows]

    rows = split(dy_ref[pl.ds(pl.multiple_of(narrow * SY, SY), SY), :])
    spread = (lax.broadcasted_iota(jnp.int32, (256, SY), 0) % SY == lax.broadcasted_iota(jnp.int32, (256, SY), 1)).astype(BF16)
    odd = narrow % 2
    other = narrow + 2 * odd - 1
    partner = narrow + 1 - 2 * odd
    chosen = (row == other * SY + col % SY).astype(BF16)
    far_ref[0], far_ref[1] = expand(rows, spread, chosen, row // SY == col // SY)
    chosen = (row == jnp.where((col // SY) % 2 == 0, narrow, partner) * SY + col % SY).astype(BF16)
    near_ref[0], near_ref[1] = expand(rows, spread[:128], chosen, row[:128] // SY == col[:128] // (2 * SY))
    rows = split(dz_ref[pl.ds(pl.multiple_of(wide * SZ, SZ), SZ), :])
    spread = (lax.broadcasted_iota(jnp.int32, (256, SZ), 0) // 8 == lax.broadcasted_iota(jnp.int32, (256, SZ), 1)).astype(BF16)
    source = lax.broadcasted_iota(jnp.int32, (512, 256), 0)
    plane = lax.broadcasted_iota(jnp.int32, (512, 256), 1) // 8
    halo = jnp.where(plane < HZ, plane - HZ, plane - HZ + SZ)
    for out_ref, offset in ((z_ref, plane), (side_ref, halo)):
        chosen = (source == wide * SZ + offset).astype(BF16)
        out_ref[0], out_ref[1] = expand(rows, spread, chosen, row % 8 == col % 8)


def prep(deriv_x, deriv_y, deriv_z):
    outs = [pltpu.VMEM((2, rows, 256), BF16) for rows in (256, 256, 256, 256, 128)]
    outs.append(jax.ShapeDtypeStruct((8, 128), F32))
    return call(prep_kernel, (deriv_x, deriv_y, deriv_z), outs, "prep", in_specs=[VMEM] * 3, out_specs=[VMEM] * 6)


def turbine_kernel(block_ref, thrust_ref, owner_ref, adj_ref, vel_ref, weight_ref, force_ref, grad_ref, ax, ay, ux, total, padded, g0, g1):
    wide, narrow = lax.axis_index("wide"), lax.axis_index("narrow")
    cells = SZ * SY
    for half in range(2):
        lanes = pl.ds(128 * half, 128)
        rows = pl.ds(cells * half, cells)
        ax[rows, :] = adj_ref[0, :, :, lanes].reshape(cells, 128)
        ay[rows, :] = adj_ref[1, :, :, lanes].reshape(cells, 128)
        ux[rows, :] = vel_ref[0, :, :, lanes].reshape(cells, 128)
    total[...] = jnp.zeros_like(total)
    padded[...] = jnp.zeros_like(padded)
    g0[...] = jnp.zeros_like(g0)
    g1[...] = jnp.zeros_like(g1)

    def turbine(t, _):
        block = block_ref[0, t]
        start_z = block // (2 * NY) - wide * SZ
        start_y = (block // 2) % NY - narrow * SY
        half = block % 2
        near = (start_z > -SZ) & (start_z < SZ) & (start_y > -2) & (start_y < SY)

        @pl.when(near)
        def _():
            padded[pl.ds(64, 64), :] = weight_ref[t]
            for line in range(2):
                y = start_y + line

                @pl.when((y >= 0) & (y < SY))
                def _():
                    w = padded[pl.ds(64 - 2 * start_z + line, SZ, stride=2), :]
                    rows = pl.ds(half * cells + y, SZ, stride=SY)
                    a, b, u = ax[rows, :], ay[rows, :], ux[rows, :]
                    size = jnp.abs(u)
                    drive = w * (u * size)
                    g0[pl.ds(t, 1), :] += jnp.sum(drive * a, axis=0, keepdims=True)
                    g1[pl.ds(t, 1), :] += jnp.sum(drive * b, axis=0, keepdims=True)
                    total[rows, :] += (thrust_ref[t] * w) * (size * a)

        return 0

    lax.fori_loop(0, TURB, turbine, 0)
    for half in range(2):
        force_ref[:, :, pl.ds(128 * half, 128)] = total[pl.ds(cells * half, cells), :].reshape(SZ, SY, 128)
    ones = jnp.ones((8, 128), F32)
    lanes_sum = lambda g: lax.dot_general(
        ones, g[...], (((1,), (1,)), ((), ())), precision=lax.Precision.HIGHEST, preferred_element_type=F32
    )
    row, col = lax.broadcasted_iota(jnp.int32, (128, 128), 0), lax.broadcasted_iota(jnp.int32, (128, 128), 1)
    owner = owner_ref[0:1, :]
    owner_col = jnp.sum(jnp.where(row == col, owner, 0), axis=1, keepdims=True)
    rank = jnp.sum(((owner_col == owner) & (row < col)).astype(jnp.int32), axis=0, keepdims=True)
    value = jnp.where(row % 2 == 0, lanes_sum(g0)[0:1], lanes_sum(g1)[0:1]) * (1.0 / math.sqrt(128.0 * 64.0))
    value = jnp.where((row < 4) & (rank == row // 2), value, 0.0)
    grad_ref[...] = lax.dot_general(
        (owner == row).astype(F32), value, (((1,), (1,)), ((), ())), precision=lax.Precision.HIGHEST, preferred_element_type=F32
    )


def turbines(blocks, thrust, owner, adjoint, velocity, weight):
    scratch = [pltpu.VMEM((2 * SZ * SY, 128), F32)] * 4 + [pltpu.VMEM((192, 128), F32)] + [pltpu.VMEM((128, 128), F32)] * 2
    outs = [pltpu.VMEM((SZ, SY, NX), F32), jax.ShapeDtypeStruct((128, 128), F32)]
    operands = (blocks, thrust, owner, adjoint, velocity, weight)
    return call(turbine_kernel, operands, outs, "turbines", 16, in_specs=[SMEM] * 2 + [VMEM] * 4, out_specs=[VMEM] * 2, scratch_shapes=scratch)


def copy_of(source, target, sem):
    return pltpu.make_async_copy(source, target, sem)


def chip_lines(one, two, c, at):
    return jnp.stack([one[c, at, :, :], two[c, at, :, :]], axis=1).reshape(256, 256)


def xz_kernel(token_ref, adj_ref, vel_ref, force_ref, x_ref, z_ref, out_ref, next_ref, tend, sems):
    next_ref[...] = token_ref[...]
    stores = []
    for yb in range(SY // 8):
        at = pl.ds(yb * 8, 8)
        field = lambda ref, c: ref[c, :, at, :].reshape(256, 256)
        x_hi, x_lo, z_hi, z_lo = x_ref[0], x_ref[1], z_ref[0], z_ref[1]

        def both(v):
            hi, lo = split(v)
            return (
                dot(hi, x_hi) + (dot(lo, x_hi) + dot(hi, x_lo)),
                dot(z_hi, hi) + (dot(z_hi, lo) + dot(z_lo, hi)),
            )

        stretch_x = jnp.zeros((256, 256), F32)
        stretch_z = jnp.zeros((256, 256), F32)
        for c in range(3):
            dx, dz = both(field(vel_ref, c))
            a = field(adj_ref, c)
            stretch_x += a * dx
            stretch_z += a * dz
        for c in range(3):
            a = field(adj_ref, c)
            dx, dz = both(a)
            total = field(vel_ref, 0) * dx + field(vel_ref, 2) * dz
            if c == 0:
                total -= stretch_x + force_ref[:, at, :].reshape(256, 256)
            if c == 2:
                total -= stretch_z
            tend[c, :, at, :] = (a + STEP * total).reshape(SZ, 8, NX)
        stores.append(copy_of(tend.at[:, :, at], out_ref.at[:, :, at], sems.at[yb]))
        stores[-1].start()
    for copy in stores:
        copy.wait()


def side_lines(up_ref, down_ref, c, at):
    return jnp.concatenate([up_ref[c, :, at, :].reshape(128, 256), down_ref[c, :, at, :].reshape(128, 256)], axis=0)


def adj_kernel(vel_ref, far_ref, up_ref, down_ref, y_ref, z_ref, old_ref, out_ref, vel, far, upper, lower, sems):
    groups = [pl.ds(8 * g, 8) for g in range(SZ // 8)]
    parts = lambda at: ((far_ref.at[:, at], far.at[:, at]), (old_ref.at[:, at], out_ref.at[:, at]), (vel_ref.at[1, at], vel.at[0, at]))
    loads = [[copy_of(*ends, sems.at[i, g]) for i, ends in enumerate(parts(at))] for g, at in enumerate(groups)]
    ends = ((vel_ref.at[2], vel.at[1]), (up_ref, upper), (down_ref, lower))
    loads.append([copy_of(*pair, sems.at[3, i]) for i, pair in enumerate(ends)])
    for copies in loads:
        for copy in copies:
            copy.start()
    for at, copies in zip(groups, loads):
        for copy in copies:
            copy.wait()
        field = lambda ref, c: ref[c, at, :, :].reshape(256, 256)
        for c in range(3):
            total = field(vel, 0) * mix(y_ref[0], y_ref[1], field(far, c))
            out_ref[c, at, :, :] = (field(out_ref, c) + STEP * total).reshape(8, SY, NX)
    for copy in loads[-1]:
        copy.wait()
    for at in groups:
        field = lambda ref, c: ref[c, :, at, :].reshape(256, 256)
        for c in range(3):
            total = field(vel, 1) * mix(z_ref[0], z_ref[1], side_lines(upper, lower, c, at))
            out_ref[c, :, at, :] = (field(out_ref, c) + STEP * total).reshape(SZ, 8, NX)


def near_kernel(before_ref, adj_ref, vel_ref, adj2_ref, vel2_ref, k_ref, old_ref, done_ref, rest_ref, token_ref, adj2, vel2, stage, sems):
    token_ref[...] = before_ref[...]
    groups = [pl.ds(4 * g, 4) for g in range(SZ // 4)]
    loads = []
    for g, at in enumerate(groups):
        loads.append((copy_of(adj2_ref.at[:, at], adj2.at[:, at], sems.at[0, g]), copy_of(vel2_ref.at[:, at], vel2.at[:, at], sems.at[1, g])))
        for copy in loads[-1]:
            copy.start()
    both = jnp.concatenate([k_ref[0], k_ref[1]], axis=0)
    stores = []
    for g, at in enumerate(groups):
        for copy in loads[g]:
            copy.wait()
        field = lambda ref, c: ref[c, at, :, :].reshape(128, 256)

        def deriv(one, two, c):
            hi, lo = split(chip_lines(one, two, c, at))
            most = dot(both, hi)
            return most[:128] + (most[128:] + dot(k_ref[0], lo))

        stretch = jnp.zeros((128, 256), F32)
        for c in range(3):
            stretch += field(adj_ref, c) * deriv(vel_ref, vel2, c)
        for c in range(3):
            total = field(vel_ref, 1) * deriv(adj_ref, adj2, c)
            if c == 1:
                total -= stretch
            total = (field(old_ref, c) + STEP * total).reshape(4, SY, NX)
            if c == 0:
                stage[at, :, :] = total
            else:
                rest_ref[c - 1, at, :, :] = total
        stores.append(copy_of(stage.at[at], done_ref.at[0, at], sems.at[2, g]))
        stores[-1].start()
    for copy in stores:
        copy.wait()


def far_kernel(token_ref, adj_ref, far_ref, k_ref, rest_ref, done_ref, out_ref, last_ref, stage, sems):
    del token_ref, done_ref
    stores = []
    for g in range(SZ // 8):
        at = pl.ds(8 * g, 8)
        field = lambda ref, c: ref[c, at, :, :].reshape(256, 256)
        stretch = jnp.zeros((256, 256), F32)
        for c in range(3):
            stretch += field(adj_ref, c) * mix(k_ref[0], k_ref[1], field(far_ref, c))
        stage[at, :, :] = (field(rest_ref, 0) - STEP * stretch).reshape(8, SY, NX)
        stores.append(copy_of(stage.at[at], out_ref.at[1, at], sems.at[g]))
        stores[-1].start()
    last_ref[...] = rest_ref[1]
    for copy in stores:
        copy.wait()


def z_kernel(adj_ref, up_ref, down_ref, k_ref, last_ref, done_ref, out_ref, token_ref, stage, sems):
    del done_ref
    token_ref[...] = jnp.zeros_like(token_ref)
    stores = []
    for yb in range(SY // 8):
        at = pl.ds(8 * yb, 8)
        field = lambda ref, c: ref[c, :, at, :].reshape(256, 256)
        stretch = jnp.zeros((256, 256), F32)
        for c in range(3):
            stretch += field(adj_ref, c) * mix(k_ref[0], k_ref[1], side_lines(up_ref, down_ref, c, at))
        stage[:, at, :] = (last_ref[:, at, :].reshape(256, 256) - STEP * stretch).reshape(SZ, 8, NX)
        stores.append(copy_of(stage.at[:, at], out_ref.at[2, :, at], sems.at[yb]))
        stores[-1].start()
    for copy in stores:
        copy.wait()


def share_kernel(terms_ref, done_ref, out_ref):
    del done_ref
    total = jnp.sum(terms_ref[...].reshape(128, 128), axis=0, keepdims=True)
    out_ref[0:1, :] = total[:, 0:2]
    out_ref[1:2, :] = total[:, 2:4]


def on_device(adjoint, velocity, deriv_x, deriv_y, deriv_z, rotor_blocks, turbine_owner, disk_weight, thrust):
    n_wide, n_narrow = lax.axis_size("wide"), lax.axis_size("narrow")
    up = [(i, i + 1) for i in range(n_wide - 1)]
    down = [(i + 1, i) for i in range(n_wide - 1)]
    chip = [(i, i ^ 1) for i in range(n_narrow)]
    across = [pair for i in range(1, n_narrow - 1, 2) for pair in ((i, i + 1), (i + 1, i))]
    barrier = lax.optimization_barrier
    shape = jax.ShapeDtypeStruct(adjoint.shape, F32)
    field = pltpu.VMEM(adjoint.shape, F32)
    dma = pltpu.SemaphoreType.DMA

    small = jax.ShapeDtypeStruct((8, 128), F32)
    far = lambda v: lax.ppermute(v, "narrow", across)
    sides = lambda upper, lower: [lax.ppermute(upper, "wide", up), lax.ppermute(lower, "wide", down)]

    first, upper, lower = barrier((adjoint, adjoint[:, HZ:], adjoint[:, :HZ]))
    adj_sides = sides(upper, lower)
    adj_far = far(first)
    near = [lax.ppermute(v, "narrow", chip) for v in (first, velocity)]
    adj, vel = resident(adjoint), resident(velocity)
    owner = jnp.broadcast_to(jnp.pad(turbine_owner, (0, 128 - TURB), constant_values=-1)[None], (8, 128))
    force, grad = turbines(rotor_blocks.T, thrust, owner, adj, vel, resident(disk_weight))
    deriv_y, grad, vel_upper, vel_lower, *near = barrier((deriv_y, grad, velocity[:, HZ:], velocity[:, :HZ], *near))
    m_x, m_z, m_side, m_far, m_near, token = prep(deriv_x, deriv_y, deriv_z)
    grad = lax.all_to_all(grad.reshape(n_wide * n_narrow, 1, 128), ("wide", "narrow"), split_axis=0, concat_axis=0, tiled=True)
    out, token = call(
        xz_kernel,
        (token, adj, vel, force, m_x, m_z),
        [pltpu.HBM(adjoint.shape, F32), small],
        "xz",
        16,
        in_specs=[VMEM] * 6,
        out_specs=[HBM, VMEM],
        scratch_shapes=[field, dma((4,))],
    )
    token, gated = barrier((token, velocity))
    vel_far = far(gated)
    out, upper, lower, adj_far, *adj_sides = barrier(
        (out, vel_upper, vel_lower, adj_far, *adj_sides)
    )

    vel_sides = sides(upper, lower)
    adj, vel = resident(adjoint), resident(velocity)
    two, side = pltpu.VMEM((2, SZ, SY, NX), F32), pltpu.VMEM((3, HZ, SY, NX), F32)
    out = call(
        adj_kernel,
        (*[in_hbm(v) for v in (velocity, adj_far, *adj_sides)], m_far, m_side, in_hbm(out)),
        field,
        "halo_adj",
        16,
        in_specs=[HBM] * 4 + [VMEM] * 2 + [HBM],
        out_specs=VMEM,
        scratch_shapes=[two, field, side, side, dma((4, 4))],
    )
    out, rest, token = call(
        near_kernel,
        (token, adj, vel, *[in_hbm(v) for v in near], m_near, out),
        [shape, pltpu.VMEM((2, SZ, SY, NX), F32), small],
        "near",
        20,
        in_specs=[VMEM] * 3 + [HBM] * 2 + [VMEM] * 2,
        out_specs=[HBM, VMEM, VMEM],
        scratch_shapes=[field, field, pltpu.VMEM((SZ, SY, NX), F32), dma((3, 8))],
    )
    token, vel_far = barrier((token, vel_far))
    plane = pltpu.VMEM((SZ, SY, NX), F32)
    out, last = call(
        far_kernel,
        (token, adj, resident(vel_far), m_far, rest, out),
        [shape, plane],
        "far_vel",
        in_specs=[VMEM] * 5 + [HBM],
        out_specs=[HBM, VMEM],
        input_output_aliases={5: 0},
        scratch_shapes=[plane, dma((4,))],
    )
    out, token = call(
        z_kernel,
        (adj, *[resident(v) for v in vel_sides], m_side, last, out),
        [shape, small],
        "z_vel",
        in_specs=[VMEM] * 5 + [HBM],
        out_specs=[HBM, VMEM],
        input_output_aliases={5: 0},
        scratch_shapes=[plane, dma((4,))],
    )
    share = call(share_kernel, (grad, token), jax.ShapeDtypeStruct((2, 2), F32), "share", in_specs=[VMEM] * 2, out_specs=VMEM)
    return out, share


def solution(mesh):
    field = P(None, "wide", "narrow", None)
    return jax.shard_map(
        on_device,
        mesh=mesh,
        in_specs=(field, field) + (P(),) * 7,
        out_specs=(field, P(("wide", "narrow"), None)),
        check_vma=False,
    )
```

```python
import math

import jax
import jax.numpy as jnp
from jax import lax
from jax.experimental import pallas as pl
from jax.experimental.pallas import tpu as pltpu
from jax.sharding import PartitionSpec as P

F32 = jnp.float32
BF16 = jnp.bfloat16
NX = 256
NY = 256
SZ = 32
SY = 32
HZ = 16
TURB = 96
STEP = 0.2
VMEM = pl.BlockSpec(memory_space=pltpu.VMEM)
SMEM = pl.BlockSpec(memory_space=pltpu.SMEM)
HBM = pl.BlockSpec(memory_space=pl.ANY)
COST = pl.CostEstimate(flops=1, transcendentals=0, bytes_accessed=1)


def resident(v):
    return pltpu.with_memory_space_constraint(v, pltpu.VMEM)


def in_hbm(v):
    return pltpu.with_memory_space_constraint(v, pltpu.HBM)


def call(kernel, operands, outs, name, limit=12, **kw):
    return pl.pallas_call(
        kernel,
        out_shape=outs,
        compiler_params=pltpu.CompilerParams(vmem_limit_bytes=limit << 20),
        cost_estimate=COST,
        name=name,
        **kw,
    )(*operands)


def split(v):
    hi = v.astype(BF16)
    lo = (v - hi.astype(F32)).astype(BF16)
    return hi, lo


def dot(a, b):
    return lax.dot_general(a, b, (((1,), (0,)), ((), ())), preferred_element_type=F32)


def mix(k_hi, k_lo, v):
    hi, lo = split(v)
    return dot(k_hi, hi) + (dot(k_hi, lo) + dot(k_lo, hi))


def iota(axis):
    return lax.broadcasted_iota(jnp.int32, (256, 256), axis)


def prep_kernel(dx_ref, dy_ref, dz_ref, x_ref, z_ref, side_ref, far_ref, near_ref, token_ref):
    token_ref[...] = jnp.zeros_like(token_ref)
    wide, narrow = lax.axis_index("wide"), lax.axis_index("narrow")
    row, col = iota(0), iota(1)
    x_ref[0], x_ref[1] = split(dx_ref[...].T)

    def expand(rows, spread, chosen, same):
        return [jnp.where(same, dot(dot(spread, half).astype(BF16), chosen), 0.0).astype(BF16) for half in rows]

    rows = split(dy_ref[pl.ds(pl.multiple_of(narrow * SY, SY), SY), :])
    spread = (lax.broadcasted_iota(jnp.int32, (256, SY), 0) % SY == lax.broadcasted_iota(jnp.int32, (256, SY), 1)).astype(BF16)
    odd = narrow % 2
    other = narrow + 2 * odd - 1
    partner = narrow + 1 - 2 * odd
    chosen = (row == other * SY + col % SY).astype(BF16)
    far_ref[0], far_ref[1] = expand(rows, spread, chosen, row // SY == col // SY)
    chosen = (row == jnp.where((col // SY) % 2 == 0, narrow, partner) * SY + col % SY).astype(BF16)
    near_ref[0], near_ref[1] = expand(rows, spread[:128], chosen, row[:128] // SY == col[:128] // (2 * SY))
    rows = split(dz_ref[pl.ds(pl.multiple_of(wide * SZ, SZ), SZ), :])
    spread = (lax.broadcasted_iota(jnp.int32, (256, SZ), 0) // 8 == lax.broadcasted_iota(jnp.int32, (256, SZ), 1)).astype(BF16)
    source = lax.broadcasted_iota(jnp.int32, (512, 256), 0)
    plane = lax.broadcasted_iota(jnp.int32, (512, 256), 1) // 8
    halo = jnp.where(plane < HZ, plane - HZ, plane - HZ + SZ)
    for out_ref, offset in ((z_ref, plane), (side_ref, halo)):
        chosen = (source == wide * SZ + offset).astype(BF16)
        out_ref[0], out_ref[1] = expand(rows, spread, chosen, row % 8 == col % 8)


def prep(deriv_x, deriv_y, deriv_z):
    outs = [pltpu.VMEM((2, rows, 256), BF16) for rows in (256, 256, 256, 256, 128)]
    outs.append(jax.ShapeDtypeStruct((8, 128), F32))
    return call(prep_kernel, (deriv_x, deriv_y, deriv_z), outs, "prep", in_specs=[VMEM] * 3, out_specs=[VMEM] * 6)


def turbine_kernel(block_ref, thrust_ref, owner_ref, adj_ref, vel_ref, weight_ref, force_ref, grad_ref, ax, ay, ux, total, padded, g0, g1):
    wide, narrow = lax.axis_index("wide"), lax.axis_index("narrow")
    cells = SZ * SY
    for half in range(2):
        lanes = pl.ds(128 * half, 128)
        rows = pl.ds(cells * half, cells)
        ax[rows, :] = adj_ref[0, :, :, lanes].reshape(cells, 128)
        ay[rows, :] = adj_ref[1, :, :, lanes].reshape(cells, 128)
        ux[rows, :] = vel_ref[0, :, :, lanes].reshape(cells, 128)
    total[...] = jnp.zeros_like(total)
    padded[...] = jnp.zeros_like(padded)
    g0[...] = jnp.zeros_like(g0)
    g1[...] = jnp.zeros_like(g1)

    def turbine(t, _):
        block = block_ref[0, t]
        start_z = block // (2 * NY) - wide * SZ
        start_y = (block // 2) % NY - narrow * SY
        half = block % 2
        near = (start_z > -SZ) & (start_z < SZ) & (start_y > -2) & (start_y < SY)

        @pl.when(near)
        def _():
            padded[pl.ds(64, 64), :] = weight_ref[t]
            for line in range(2):
                y = start_y + line

                @pl.when((y >= 0) & (y < SY))
                def _():
                    w = padded[pl.ds(64 - 2 * start_z + line, SZ, stride=2), :]
                    rows = pl.ds(half * cells + y, SZ, stride=SY)
                    a, b, u = ax[rows, :], ay[rows, :], ux[rows, :]
                    size = jnp.abs(u)
                    drive = w * (u * size)
                    g0[pl.ds(t, 1), :] += jnp.sum(drive * a, axis=0, keepdims=True)
                    g1[pl.ds(t, 1), :] += jnp.sum(drive * b, axis=0, keepdims=True)
                    total[rows, :] += (thrust_ref[t] * w) * (size * a)

        return 0

    lax.fori_loop(0, TURB, turbine, 0)
    for half in range(2):
        force_ref[:, :, pl.ds(128 * half, 128)] = total[pl.ds(cells * half, cells), :].reshape(SZ, SY, 128)
    ones = jnp.ones((8, 128), F32)
    lanes_sum = lambda g: lax.dot_general(
        ones, g[...], (((1,), (1,)), ((), ())), precision=lax.Precision.HIGHEST, preferred_element_type=F32
    )
    row, col = lax.broadcasted_iota(jnp.int32, (128, 128), 0), lax.broadcasted_iota(jnp.int32, (128, 128), 1)
    owner = owner_ref[0:1, :]
    owner_col = jnp.sum(jnp.where(row == col, owner, 0), axis=1, keepdims=True)
    rank = jnp.sum(((owner_col == owner) & (row < col)).astype(jnp.int32), axis=0, keepdims=True)
    value = jnp.where(row % 2 == 0, lanes_sum(g0)[0:1], lanes_sum(g1)[0:1]) * (1.0 / math.sqrt(128.0 * 64.0))
    value = jnp.where((row < 4) & (rank == row // 2), value, 0.0)
    grad_ref[...] = lax.dot_general(
        (owner == row).astype(F32), value, (((1,), (1,)), ((), ())), precision=lax.Precision.HIGHEST, preferred_element_type=F32
    )


def turbines(blocks, thrust, owner, adjoint, velocity, weight):
    scratch = [pltpu.VMEM((2 * SZ * SY, 128), F32)] * 4 + [pltpu.VMEM((192, 128), F32)] + [pltpu.VMEM((128, 128), F32)] * 2
    outs = [pltpu.VMEM((SZ, SY, NX), F32), jax.ShapeDtypeStruct((128, 128), F32)]
    operands = (blocks, thrust, owner, adjoint, velocity, weight)
    return call(turbine_kernel, operands, outs, "turbines", 16, in_specs=[SMEM] * 2 + [VMEM] * 4, out_specs=[VMEM] * 2, scratch_shapes=scratch)


def copy_of(source, target, sem):
    return pltpu.make_async_copy(source, target, sem)


def chip_lines(one, two, c, at):
    return jnp.stack([one[c, at, :, :], two[c, at, :, :]], axis=1).reshape(256, 256)


def xz_kernel(token_ref, adj_ref, vel_ref, force_ref, x_ref, z_ref, out_ref, next_ref, tend, sems):
    next_ref[...] = token_ref[...]
    stores = []
    for yb in range(SY // 8):
        at = pl.ds(yb * 8, 8)
        field = lambda ref, c: ref[c, :, at, :].reshape(256, 256)
        x_hi, x_lo, z_hi, z_lo = x_ref[0], x_ref[1], z_ref[0], z_ref[1]

        def both(v):
            hi, lo = split(v)
            return (
                dot(hi, x_hi) + (dot(lo, x_hi) + dot(hi, x_lo)),
                dot(z_hi, hi) + (dot(z_hi, lo) + dot(z_lo, hi)),
            )

        stretch_x = jnp.zeros((256, 256), F32)
        stretch_z = jnp.zeros((256, 256), F32)
        for c in range(3):
            dx, dz = both(field(vel_ref, c))
            a = field(adj_ref, c)
            stretch_x += a * dx
            stretch_z += a * dz
        for c in range(3):
            a = field(adj_ref, c)
            dx, dz = both(a)
            total = field(vel_ref, 0) * dx + field(vel_ref, 2) * dz
            if c == 0:
                total -= stretch_x + force_ref[:, at, :].reshape(256, 256)
            if c == 2:
                total -= stretch_z
            tend[c, :, at, :] = (a + STEP * total).reshape(SZ, 8, NX)
        stores.append(copy_of(tend.at[:, :, at], out_ref.at[:, :, at], sems.at[yb]))
        stores[-1].start()
    for copy in stores:
        copy.wait()


def side_lines(up_ref, down_ref, c, at):
    return jnp.concatenate([up_ref[c, :, at, :].reshape(128, 256), down_ref[c, :, at, :].reshape(128, 256)], axis=0)


def adj_kernel(vel_ref, far_ref, up_ref, down_ref, y_ref, z_ref, old_ref, out_ref, vel, far, upper, lower, sems):
    groups = [pl.ds(8 * g, 8) for g in range(SZ // 8)]
    parts = lambda at: ((far_ref.at[:, at], far.at[:, at]), (old_ref.at[:, at], out_ref.at[:, at]), (vel_ref.at[1, at], vel.at[0, at]))
    loads = [[copy_of(*ends, sems.at[i, g]) for i, ends in enumerate(parts(at))] for g, at in enumerate(groups)]
    ends = ((vel_ref.at[2], vel.at[1]), (up_ref, upper), (down_ref, lower))
    loads.append([copy_of(*pair, sems.at[3, i]) for i, pair in enumerate(ends)])
    for copies in loads:
        for copy in copies:
            copy.start()
    for at, copies in zip(groups, loads):
        for copy in copies:
            copy.wait()
        field = lambda ref, c: ref[c, at, :, :].reshape(256, 256)
        for c in range(3):
            total = field(vel, 0) * mix(y_ref[0], y_ref[1], field(far, c))
            out_ref[c, at, :, :] = (field(out_ref, c) + STEP * total).reshape(8, SY, NX)
    for copy in loads[-1]:
        copy.wait()
    for at in groups:
        field = lambda ref, c: ref[c, :, at, :].reshape(256, 256)
        for c in range(3):
            total = field(vel, 1) * mix(z_ref[0], z_ref[1], side_lines(upper, lower, c, at))
            out_ref[c, :, at, :] = (field(out_ref, c) + STEP * total).reshape(SZ, 8, NX)


def near_kernel(before_ref, adj_ref, vel_ref, adj2_ref, vel2_ref, k_ref, old_ref, done_ref, rest_ref, token_ref, adj2, vel2, stage, sems):
    token_ref[...] = before_ref[...]
    groups = [pl.ds(4 * g, 4) for g in range(SZ // 4)]
    loads = []
    for g, at in enumerate(groups):
        loads.append((copy_of(adj2_ref.at[:, at], adj2.at[:, at], sems.at[0, g]), copy_of(vel2_ref.at[:, at], vel2.at[:, at], sems.at[1, g])))
        for copy in loads[-1]:
            copy.start()
    both = jnp.concatenate([k_ref[0], k_ref[1]], axis=0)
    stores = []
    for g, at in enumerate(groups):
        for copy in loads[g]:
            copy.wait()
        field = lambda ref, c: ref[c, at, :, :].reshape(128, 256)

        def deriv(one, two, c):
            hi, lo = split(chip_lines(one, two, c, at))
            most = dot(both, hi)
            return most[:128] + (most[128:] + dot(k_ref[0], lo))

        stretch = jnp.zeros((128, 256), F32)
        for c in range(3):
            stretch += field(adj_ref, c) * deriv(vel_ref, vel2, c)
        for c in range(3):
            total = field(vel_ref, 1) * deriv(adj_ref, adj2, c)
            if c == 1:
                total -= stretch
            total = (field(old_ref, c) + STEP * total).reshape(4, SY, NX)
            if c == 0:
                stage[at, :, :] = total
            else:
                rest_ref[c - 1, at, :, :] = total
        stores.append(copy_of(stage.at[at], done_ref.at[0, at], sems.at[2, g]))
        stores[-1].start()
    for copy in stores:
        copy.wait()


def far_kernel(token_ref, adj_ref, far_ref, k_ref, rest_ref, done_ref, out_ref, last_ref, stage, sems):
    del token_ref, done_ref
    stores = []
    for g in range(SZ // 8):
        at = pl.ds(8 * g, 8)
        field = lambda ref, c: ref[c, at, :, :].reshape(256, 256)
        stretch = jnp.zeros((256, 256), F32)
        for c in range(3):
            stretch += field(adj_ref, c) * mix(k_ref[0], k_ref[1], field(far_ref, c))
        stage[at, :, :] = (field(rest_ref, 0) - STEP * stretch).reshape(8, SY, NX)
        stores.append(copy_of(stage.at[at], out_ref.at[1, at], sems.at[g]))
        stores[-1].start()
    last_ref[...] = rest_ref[1]
    for copy in stores:
        copy.wait()


def z_kernel(adj_ref, up_ref, down_ref, k_ref, last_ref, done_ref, out_ref, token_ref, upper, lower, stage, sems):
    del done_ref
    token_ref[...] = jnp.zeros_like(token_ref)
    groups = [pl.ds(8 * g, 8) for g in range(SY // 8)]
    loads = []
    for g, at in enumerate(groups):
        loads.append((copy_of(up_ref.at[:, :, at], upper.at[:, :, at], sems.at[0, g]), copy_of(down_ref.at[:, :, at], lower.at[:, :, at], sems.at[1, g])))
        for copy in loads[-1]:
            copy.start()
    stores = []
    for g, at in enumerate(groups):
        for copy in loads[g]:
            copy.wait()
        field = lambda ref, c: ref[c, :, at, :].reshape(256, 256)
        stretch = jnp.zeros((256, 256), F32)
        for c in range(3):
            stretch += field(adj_ref, c) * mix(k_ref[0], k_ref[1], side_lines(upper, lower, c, at))
        stage[:, at, :] = (last_ref[:, at, :].reshape(256, 256) - STEP * stretch).reshape(SZ, 8, NX)
        stores.append(copy_of(stage.at[:, at], out_ref.at[2, :, at], sems.at[2, g]))
        stores[-1].start()
    for copy in stores:
        copy.wait()


def share_kernel(terms_ref, done_ref, out_ref):
    del done_ref
    total = jnp.sum(terms_ref[...].reshape(128, 128), axis=0, keepdims=True)
    out_ref[0:1, :] = total[:, 0:2]
    out_ref[1:2, :] = total[:, 2:4]


def on_device(adjoint, velocity, deriv_x, deriv_y, deriv_z, rotor_blocks, turbine_owner, disk_weight, thrust):
    n_wide, n_narrow = lax.axis_size("wide"), lax.axis_size("narrow")
    up = [(i, i + 1) for i in range(n_wide - 1)]
    down = [(i + 1, i) for i in range(n_wide - 1)]
    chip = [(i, i ^ 1) for i in range(n_narrow)]
    across = [pair for i in range(1, n_narrow - 1, 2) for pair in ((i, i + 1), (i + 1, i))]
    barrier = lax.optimization_barrier
    shape = jax.ShapeDtypeStruct(adjoint.shape, F32)
    field = pltpu.VMEM(adjoint.shape, F32)
    dma = pltpu.SemaphoreType.DMA

    small = jax.ShapeDtypeStruct((8, 128), F32)
    far = lambda v: lax.ppermute(v, "narrow", across)
    sides = lambda upper, lower: [lax.ppermute(upper, "wide", up), lax.ppermute(lower, "wide", down)]

    first, upper, lower = barrier((adjoint, adjoint[:, HZ:], adjoint[:, :HZ]))
    adj_sides = sides(upper, lower)
    adj_far = far(first)
    near = [lax.ppermute(v, "narrow", chip) for v in (first, velocity)]
    adj, vel = resident(adjoint), resident(velocity)
    owner = jnp.broadcast_to(jnp.pad(turbine_owner, (0, 128 - TURB), constant_values=-1)[None], (8, 128))
    force, grad = turbines(rotor_blocks.T, thrust, owner, adj, vel, resident(disk_weight))
    deriv_y, grad, vel_upper, vel_lower, *near = barrier((deriv_y, grad, velocity[:, HZ:], velocity[:, :HZ], *near))
    m_x, m_z, m_side, m_far, m_near, token = prep(deriv_x, deriv_y, deriv_z)
    grad = lax.all_to_all(grad.reshape(n_wide * n_narrow, 1, 128), ("wide", "narrow"), split_axis=0, concat_axis=0, tiled=True)
    out, token = call(
        xz_kernel,
        (token, adj, vel, force, m_x, m_z),
        [pltpu.HBM(adjoint.shape, F32), small],
        "xz",
        16,
        in_specs=[VMEM] * 6,
        out_specs=[HBM, VMEM],
        scratch_shapes=[field, dma((4,))],
    )
    token, gated = barrier((token, velocity))
    vel_far = far(gated)
    out, upper, lower, adj_far, *adj_sides = barrier(
        (out, vel_upper, vel_lower, adj_far, *adj_sides)
    )

    vel_sides = sides(upper, lower)
    adj, vel = resident(adjoint), resident(velocity)
    two, side = pltpu.VMEM((2, SZ, SY, NX), F32), pltpu.VMEM((3, HZ, SY, NX), F32)
    out = call(
        adj_kernel,
        (*[in_hbm(v) for v in (velocity, adj_far, *adj_sides)], m_far, m_side, in_hbm(out)),
        field,
        "halo_adj",
        16,
        in_specs=[HBM] * 4 + [VMEM] * 2 + [HBM],
        out_specs=VMEM,
        scratch_shapes=[two, field, side, side, dma((4, 4))],
    )
    out, rest, token = call(
        near_kernel,
        (token, adj, vel, *[in_hbm(v) for v in near], m_near, out),
        [shape, pltpu.VMEM((2, SZ, SY, NX), F32), small],
        "near",
        20,
        in_specs=[VMEM] * 3 + [HBM] * 2 + [VMEM] * 2,
        out_specs=[HBM, VMEM, VMEM],
        scratch_shapes=[field, field, pltpu.VMEM((SZ, SY, NX), F32), dma((3, 8))],
    )
    token, vel_far = barrier((token, vel_far))
    plane = pltpu.VMEM((SZ, SY, NX), F32)
    out, last = call(
        far_kernel,
        (token, adj, resident(vel_far), m_far, rest, out),
        [shape, plane],
        "far_vel",
        in_specs=[VMEM] * 5 + [HBM],
        out_specs=[HBM, VMEM],
        input_output_aliases={5: 0},
        scratch_shapes=[plane, dma((4,))],
    )
    out, token = call(
        z_kernel,
        (adj, *[in_hbm(v) for v in vel_sides], m_side, last, out),
        [shape, small],
        "z_vel",
        in_specs=[VMEM] + [HBM] * 2 + [VMEM] * 2 + [HBM],
        out_specs=[HBM, VMEM],
        input_output_aliases={5: 0},
        scratch_shapes=[side, side, plane, dma((3, 4))],
    )
    share = call(share_kernel, (grad, token), jax.ShapeDtypeStruct((2, 2), F32), "share", in_specs=[VMEM] * 2, out_specs=VMEM)
    return out, share


def solution(mesh):
    field = P(None, "wide", "narrow", None)
    return jax.shard_map(
        on_device,
        mesh=mesh,
        in_specs=(field, field) + (P(),) * 7,
        out_specs=(field, P(("wide", "narrow"), None)),
        check_vma=False,
    )
```
